128 devices in a mesh: row: 8 (over z_hi, y), col: 16 (over z_lo, x, core).
Axes of the slice: x: 4, y: 4, z: 4 (z_hi: 2, z_lo: 2; z = z_hi * 2 + z_lo), core: 2. Of those that a mesh axis runs over, the one named last changes fastest.
Arguments:
- object_field: float32 [2, 4096, 8192], P(None, 'row', 'col'), may hold values from -5 to 5
- probe: float32 [2, 8, 256, 256], replicated, may hold values from -2.5 to 2.5
- intensity: float32 [256, 256, 256], P(('row', 'col')), may hold values from 0.5 to 4
- row_offset: int32 [256], P(('row', 'col')), may hold values from 0 to 511
- col_offset: int32 [256], P(('row', 'col')), may hold values from 0 to 511
- live: int32 [256], P(('row', 'col')), may hold values 0 or 1
Outputs:
- object_grad: float32 [2, 4096, 8192], P(None, 'row', 'col')
- probe_grad: float32 [2, 8, 256, 256], replicated
The draws below stay inside these ranges and needn't reach their ends.
All inputs are finite; a program needn't handle non-finite values. No bound on the sum of `live` on one device may be relied on, other than what follows from the above.
Results may differ from the reference program's by a relative error of at most 0.0003.
Values sent between devices are 32-bit elements; how exact they have to be, the bound alone decides.
A program may use at most 128 MiB of HBM per device.

```python
import jax
import jax.numpy as jnp
from jax import lax

W = 256
MODES = 8
TR = 512
TC = 512
NR = 4096
NC = 8192
NPAT = 256
N_ROW = 8
N_COL = 16


def touch_ends(result, key, low, high):
    shape = result.shape
    place = [jax.random.randint(jax.random.fold_in(key, axis), (), 0, shape[axis]) for axis in range(len(shape))]
    result = result.at[tuple(place)].set(low)
    longest = shape.index(max(shape))
    place[longest] = (place[longest] + 1) % shape[longest]
    return result.at[tuple(place)].set(high)


def steps_of(stream_key, dims, pieces, least, high):
    def one(position, blocks):
        heights = jax.random.uniform(jax.random.fold_in(jax.random.fold_in(stream_key, 6), position), (blocks,), jnp.float32, least / len(pieces), high / len(pieces))
        return jnp.repeat(jnp.exp(heights), dims[position] // blocks).reshape((-1,) + (1,) * (len(dims) - position - 1))

    loudness = one(*pieces[0])
    for cut in pieces[1:]:
        loudness = loudness * one(*cut)
    return loudness


def bell_draw(own_key, shape, scale, limit, pieces=(), kind=jnp.bfloat16):
    values = jax.random.normal(own_key, shape, jnp.float32) * scale
    if len(pieces) > 0:
        values = steps_of(own_key, shape, pieces, -0.22, 0.18) * values
    return jnp.clip(values, min=-limit, max=limit).astype(kind)


def setup_inputs(seed: int = 0) -> dict:
    streams_of = jax.random.split(jax.random.key(seed), 7)
    return {
        "object_field": bell_draw(streams_of[0], (2, NR, NC), 0.7, 5.0, ((1, 8), (2, 16)), jnp.float32),
        "probe": bell_draw(streams_of[1], (2, MODES, W, W), 0.35, 2.5, (), jnp.float32),
        "intensity": jnp.clip(0.5 + 3.5 * jax.random.uniform(streams_of[2], (NPAT, W, W), jnp.float32) ** steps_of(streams_of[2], (NPAT, W, W), ((0, 128),), -0.2, 0.2), 0.5, 4.0),
        "row_offset": touch_ends(jax.random.randint(streams_of[3], (NPAT,), 0, TR), jax.random.fold_in(streams_of[3], 1), 0, TR - 1).astype(jnp.int32),
        "col_offset": touch_ends(jax.random.randint(streams_of[4], (NPAT,), 0, TC), jax.random.fold_in(streams_of[4], 1), 0, TC - 1).astype(jnp.int32),
        "live": touch_ends((jax.random.randint(streams_of[5], (NPAT,), 0, 4) < 3).astype(jnp.int32), jax.random.fold_in(streams_of[5], 1), 0, 1),
    }


smoothing = 0.25

def reference(object_field, probe, intensity, row_offset, col_offset, live):
    width = probe.shape[-1]
    total_rows = object_field.shape[1]
    total_cols = object_field.shape[2]
    per_device = intensity.shape[0] // (N_ROW * N_COL)
    padded = jnp.pad(object_field, ((0, 0), (0, width), (0, width)))
    probe_re = probe[0]
    probe_im = probe[1]
    live_float = live.astype(jnp.float32)

    def one_pattern(carry, index):
        grad_object, grad_probe = carry
        block = index // per_device
        top = (block // N_COL * TR + row_offset[index]).astype(jnp.int32)
        left = (block % N_COL * TC + col_offset[index]).astype(jnp.int32)
        anchor = jnp.zeros((), jnp.int32)
        patch = lax.dynamic_slice(padded, (anchor, top, left), (2, width, width))
        patch_re = patch[0][None]
        patch_im = patch[1][None]
        exit_re = probe_re * patch_re - probe_im * patch_im
        exit_im = probe_re * patch_im + probe_im * patch_re
        spectrum = jnp.fft.fft2(lax.complex(exit_re, exit_im), norm='ortho')
        spec_re = jnp.real(spectrum)
        spec_im = jnp.imag(spectrum)
        amplitude = jnp.sqrt(lax.optimization_barrier(jnp.sum(spec_re * spec_re + spec_im * spec_im, axis=0)) + smoothing)
        factor = (1.0 - jnp.sqrt(intensity[index]) / amplitude) * live_float[index]
        back = jnp.fft.ifft2(lax.complex(spec_re * factor, spec_im * factor), norm='ortho')
        chi_re = jnp.real(back)
        chi_im = jnp.imag(back)
        obj_re = lax.optimization_barrier(jnp.sum(probe_re * chi_re + probe_im * chi_im, axis=0))
        obj_im = lax.optimization_barrier(jnp.sum(probe_re * chi_im - probe_im * chi_re, axis=0))
        contrib = jnp.stack([obj_re, obj_im])
        current = lax.dynamic_slice(grad_object, (anchor, top, left), (2, width, width))
        grad_object = lax.dynamic_update_slice(grad_object, current + contrib, (anchor, top, left))
        pro_re = patch_re * chi_re + patch_im * chi_im
        pro_im = patch_re * chi_im - patch_im * chi_re
        grad_probe = grad_probe + jnp.stack([pro_re, pro_im])
        return ((grad_object, grad_probe), None)
    start = (jnp.zeros_like(padded), jnp.zeros_like(probe))
    indices = jnp.arange(intensity.shape[0], dtype=jnp.int32)
    (grad_object, grad_probe), _ = lax.scan(one_pattern, start, indices)
    return (grad_object[:, :total_rows, :total_cols], grad_probe)
```

```python
import functools
import jax
import jax.numpy as jnp
import numpy as np
from jax import lax
from jax.experimental import pallas as pl
from jax.experimental.pallas import tpu as pltpu
from jax.sharding import PartitionSpec as P

BF = jnp.bfloat16
F32 = jnp.float32
W, MODES, TILE, EXT, HALF = 256, 8, 512, 768, 128


def split_np(m):
    hi = m.astype(np.float32).astype(jnp.bfloat16)
    lo = (m - hi.astype(np.float64)).astype(np.float32).astype(jnp.bfloat16)
    return hi, lo


def tables():
    n = np.arange(HALF)
    out = []
    for odd in (0, 1):
        k = 2 * np.arange(HALF) + odd
        phase = 2.0 * np.pi * ((k[:, None] * n[None, :]) % W) / W
        c, s = np.cos(phase) / 16.0, np.sin(phase) / 16.0
        m = np.block([[c, s], [-s, c]])
        for t in (m, m.T):
            out.extend(split_np(t))
    return np.stack(out)


def column_order():
    q = np.zeros((W, W), np.float32)
    for j in range(HALF):
        q[2 * j, j] = 1.0
        q[2 * j + 1, HALF + j] = 1.0
    return np.stack([q, q.T]).astype(jnp.bfloat16)


def parts(x):
    hi = x.astype(BF)
    lo = (x - hi.astype(F32)).astype(BF)
    return hi, lo


def dot(a, b):
    return jnp.dot(a, b, preferred_element_type=F32)


def left(tab, i, data):
    hi, lo = parts(data)
    return dot(tab[i], hi) + dot(tab[i + 1], hi) + dot(tab[i], lo)


def right(data, tab, i):
    hi, lo = parts(data)
    return dot(hi, tab[i]) + dot(hi, tab[i + 1]) + dot(lo, tab[i])


ME, MET, MO, MOT = 0, 2, 4, 6


def transform(re, im, tab):
    even = jnp.concatenate([re[:HALF] + re[HALF:], im[:HALF] + im[HALF:]], 0)
    odd = jnp.concatenate([re[:HALF] - re[HALF:], im[:HALF] - im[HALF:]], 0)
    ye = left(tab, ME, even)
    yo = left(tab, MO, odd)
    a = jnp.concatenate([
        jnp.concatenate([y[:HALF, :HALF] + y[:HALF, HALF:], y[HALF:, :HALF] + y[HALF:, HALF:]], 1) for y in (ye, yo)], 0)
    b = jnp.concatenate([
        jnp.concatenate([y[:HALF, :HALF] - y[:HALF, HALF:], y[HALF:, :HALF] - y[HALF:, HALF:]], 1) for y in (ye, yo)], 0)
    return right(a, tab, MET), right(b, tab, MOT)


def inverse(fe, fo, tab):
    ge = right(fe, tab, ME)
    go = right(fo, tab, MO)
    p, q = ge + go, ge - go
    even = jnp.concatenate([
        jnp.concatenate([p[:HALF, :HALF], q[:HALF, :HALF]], 1),
        jnp.concatenate([p[:HALF, HALF:], q[:HALF, HALF:]], 1)], 0)
    odd = jnp.concatenate([
        jnp.concatenate([p[HALF:, :HALF], q[HALF:, :HALF]], 1),
        jnp.concatenate([p[HALF:, HALF:], q[HALF:, HALF:]], 1)], 0)
    a = left(tab, MET, even)
    b = left(tab, MOT, odd)
    s, d = a + b, a - b
    return jnp.concatenate([s[:HALF], d[:HALF]], 0), jnp.concatenate([s[HALF:], d[HALF:]], 0)


def lanes_left(blocks, shift):
    lane = lax.broadcasted_iota(jnp.int32, blocks[0].shape, 1)
    turned = [pltpu.roll(x, lax.rem(HALF - shift, HALF), 1) for x in blocks]
    keep = lane < HALF - shift
    return [jnp.where(keep, turned[j], turned[j + 1]) for j in range(len(blocks) - 1)]


def lanes_right(blocks, shift):
    lane = lax.broadcasted_iota(jnp.int32, blocks[0].shape, 1)
    turned = [pltpu.roll(x, shift, 1) for x in blocks]
    turned = [jnp.zeros_like(blocks[0])] + turned + [jnp.zeros_like(blocks[0])]
    keep = lane >= shift
    return [jnp.where(keep, turned[j + 1], turned[j]) for j in range(len(blocks) + 1)]


def compute_kernel(top_ref, col_ref, live_ref, obj_hbm, low_hbm, right_hbm, probe_ref, int_ref, tab, perm_ref,
                   gmain_ref, gright_ref, pg_ref, ext, grad, patch, spec, contrib, amp, sems):
    copies = [
        pltpu.make_async_copy(obj_hbm, ext.at[:, pl.ds(0, TILE), pl.ds(0, TILE)], sems.at[0]),
        pltpu.make_async_copy(low_hbm, ext.at[:, pl.ds(TILE, W), pl.ds(0, TILE)], sems.at[1]),
        pltpu.make_async_copy(right_hbm, ext.at[:, :, pl.ds(TILE, W)], sems.at[2]),
    ]
    for c in copies:
        c.start()
    grad[...] = jnp.zeros_like(grad)
    contrib[...] = jnp.zeros_like(contrib)
    amp[...] = jnp.zeros_like(amp)
    for c in copies:
        c.wait()
    for k in range(2):
        t = top_ref[k]
        l = col_ref[k]
        base = pl.multiple_of(l // HALF * HALF, HALF)
        start = pl.multiple_of(t // 8 * 8, 8)
        for c in range(2):
            rows = ext[c, pl.ds(start, W + 8), pl.ds(base, 3 * HALF)]
            rows = pltpu.roll(rows, W + 8 - (t - start), 0)[:W]
            got = lanes_left([rows[:, j * HALF:(j + 1) * HALF] for j in range(3)], l - base)
            patch[k, c] = jnp.concatenate(got, 1)

    def forward(m, carry):
        pr, pi = probe_ref[0, m], probe_ref[1, m]
        for k in range(2):
            o_r, o_i = patch[k, 0], patch[k, 1]
            fe, fo = transform(pr * o_r - pi * o_i, pr * o_i + pi * o_r, tab)
            spec[k, m, 0] = fe
            spec[k, m, 1] = fo
            fe2, fo2 = fe * fe, fo * fo
            amp[k] += jnp.concatenate([fe2[:, :HALF] + fe2[:, HALF:], fo2[:, :HALF] + fo2[:, HALF:]], 1)
        return carry

    lax.fori_loop(0, MODES, forward, 0)

    for k in range(2):
        hi, lo = parts(jnp.sqrt(int_ref[k]))
        hi, lo = dot(perm_ref[1], hi).astype(BF), dot(perm_ref[1], lo).astype(BF)
        root = dot(hi, perm_ref[0]) + dot(lo, perm_ref[0])
        alive = live_ref[k].astype(F32)
        amp[k] = (1.0 - root / jnp.sqrt(amp[k] + 0.25)) * alive

    def backward(m, carry):
        pr, pi = probe_ref[0, m], probe_ref[1, m]
        gr = gi = None
        for k in range(2):
            o_r, o_i = patch[k, 0], patch[k, 1]
            f = amp[k]
            fe, fo = f[:, :HALF], f[:, HALF:]
            chi_r, chi_i = inverse(spec[k, m, 0] * jnp.concatenate([fe, fe], 1), spec[k, m, 1] * jnp.concatenate([fo, fo], 1), tab)
            contrib[k, 0] += pr * chi_r + pi * chi_i
            contrib[k, 1] += pr * chi_i - pi * chi_r
            qr = o_r * chi_r + o_i * chi_i
            qi = o_r * chi_i - o_i * chi_r
            gr = qr if gr is None else gr + qr
            gi = qi if gi is None else gi + qi
        pg_ref[0, m] = gr
        pg_ref[1, m] = gi
        return carry

    lax.fori_loop(0, MODES, backward, 0)

    for k in range(2):
        t = top_ref[k]
        l = col_ref[k]
        base = pl.multiple_of(l // HALF * HALF, HALF)
        start = pl.multiple_of(t // 8 * 8, 8)
        for c in range(2):
            g = contrib[k, c]
            wide = jnp.concatenate(lanes_right([g[:, :HALF], g[:, HALF:]], l - base), 1)
            wide = pltpu.roll(jnp.concatenate([wide, jnp.zeros((8, 3 * HALF), F32)], 0), t - start, 0)
            grad[c, pl.ds(start, W + 8), pl.ds(base, 3 * HALF)] += wide
    out = [
        pltpu.make_async_copy(grad.at[:, :, pl.ds(0, TILE)], gmain_ref, sems.at[0]),
        pltpu.make_async_copy(grad.at[:, :, pl.ds(TILE, W)], gright_ref, sems.at[1]),
    ]
    for c in out:
        c.start()
    for c in out:
        c.wait()


def compute(top, col, live, obj, low, rgt, probe, intensity):
    tab = jnp.asarray(tables())
    perm = jnp.asarray(column_order())
    smem = pl.BlockSpec(memory_space=pltpu.SMEM)
    vmem = pl.BlockSpec(memory_space=pltpu.VMEM)
    hbm = pl.BlockSpec(memory_space=pl.ANY)
    return pl.pallas_call(
        compute_kernel,
        out_shape=(
            jax.ShapeDtypeStruct((2, EXT, TILE), F32),
            jax.ShapeDtypeStruct((2, EXT, W), F32),
            jax.ShapeDtypeStruct((2, MODES, W, W), F32),
        ),
        in_specs=[smem, smem, smem, hbm, hbm, hbm, vmem, vmem, vmem, vmem],
        out_specs=(hbm, hbm, vmem),
        scratch_shapes=[
            pltpu.VMEM((2, EXT, EXT), F32),
            pltpu.VMEM((2, EXT, EXT), F32),
            pltpu.VMEM((2, 2, W, W), F32),
            pltpu.VMEM((2, MODES, 2, W, W), F32),
            pltpu.VMEM((2, 2, W, W), F32),
            pltpu.VMEM((2, W, W), F32),
            pltpu.SemaphoreType.DMA((3,)),
        ],
        compiler_params=pltpu.CompilerParams(vmem_limit_bytes=60 * 1024 * 1024),
        name="ptycho",
    )(top, col, live, obj, low, rgt, probe, intensity, tab, perm)


def along(array, axis, by):
    devices = lax.axis_size(axis)
    pairs = [(i, i + by) for i in range(devices) if 0 <= i + by < devices]
    return lax.ppermute(array, axis, pairs)


def shards(object_field, probe, intensity, row_offset, col_offset, live):
    low = along(object_field[:, :W, :], "row", -1)
    rgt = along(jnp.concatenate([object_field[:, :, :W], low[:, :, :W]], axis=1), "col", -1)
    gmain, gright, partial_probe = compute(row_offset, col_offset, live, object_field, low, rgt, probe, intensity)
    probe_grad = lax.psum(partial_probe, ("row", "col"))
    back = along(gright, "col", 1)
    gmain = gmain.at[:, :, :W].add(back)
    down = along(gmain[:, TILE:, :], "row", 1)
    object_grad = gmain[:, :TILE, :].at[:, :W, :].add(down)
    return (object_grad, probe_grad)


def solution(mesh):
    in_specs = (
        P(None, "row", "col"),
        P(),
        P(("row", "col"), None, None),
        P(("row", "col")),
        P(("row", "col")),
        P(("row", "col")),
    )
    out_specs = (P(None, "row", "col"), P())
    return jax.shard_map(shards, mesh=mesh, in_specs=in_specs, out_specs=out_specs, check_vma=False)
```

```python
import functools
import jax
import jax.numpy as jnp
import numpy as np
from jax import lax
from jax.experimental import pallas as pl
from jax.experimental.pallas import tpu as pltpu
from jax.sharding import PartitionSpec as P

BF = jnp.bfloat16
F32 = jnp.float32
W, MODES, TILE, EXT, HALF = 256, 8, 512, 768, 128


def split_np(m):
    hi = m.astype(np.float32).astype(jnp.bfloat16)
    lo = (m - hi.astype(np.float64)).astype(np.float32).astype(jnp.bfloat16)
    return hi, lo


def tables():
    n = np.arange(HALF)
    out = []
    for odd in (0, 1):
        k = 2 * np.arange(HALF) + odd
        phase = 2.0 * np.pi * ((k[:, None] * n[None, :]) % W) / W
        c, s = np.cos(phase) / 16.0, np.sin(phase) / 16.0
        m = np.block([[c, s], [-s, c]])
        for t in (m, m.T):
            out.extend(split_np(t))
    return np.stack(out)


def column_order():
    q = np.zeros((W, W), np.float32)
    for j in range(HALF):
        q[2 * j, j] = 1.0
        q[2 * j + 1, HALF + j] = 1.0
    return np.stack([q, q.T]).astype(jnp.bfloat16)


def parts(x):
    hi = x.astype(BF)
    lo = (x - hi.astype(F32)).astype(BF)
    return hi, lo


def dot(a, b):
    return jnp.dot(a, b, preferred_element_type=F32)


def left(tab, i, data):
    hi, lo = parts(data)
    return dot(tab[i], hi) + dot(tab[i + 1], hi) + dot(tab[i], lo)


def right(data, tab, i):
    hi, lo = parts(data)
    return dot(hi, tab[i]) + dot(hi, tab[i + 1]) + dot(lo, tab[i])


ME, MET, MO, MOT = 0, 2, 4, 6


def transform(re, im, tab):
    even = jnp.concatenate([re[:HALF] + re[HALF:], im[:HALF] + im[HALF:]], 0)
    odd = jnp.concatenate([re[:HALF] - re[HALF:], im[:HALF] - im[HALF:]], 0)
    ye = left(tab, ME, even)
    yo = left(tab, MO, odd)
    a = jnp.concatenate([
        jnp.concatenate([y[:HALF, :HALF] + y[:HALF, HALF:], y[HALF:, :HALF] + y[HALF:, HALF:]], 1) for y in (ye, yo)], 0)
    b = jnp.concatenate([
        jnp.concatenate([y[:HALF, :HALF] - y[:HALF, HALF:], y[HALF:, :HALF] - y[HALF:, HALF:]], 1) for y in (ye, yo)], 0)
    return right(a, tab, MET), right(b, tab, MOT)


def inverse(fe, fo, tab):
    ge = right(fe, tab, ME)
    go = right(fo, tab, MO)
    p, q = ge + go, ge - go
    even = jnp.concatenate([
        jnp.concatenate([p[:HALF, :HALF], q[:HALF, :HALF]], 1),
        jnp.concatenate([p[:HALF, HALF:], q[:HALF, HALF:]], 1)], 0)
    odd = jnp.concatenate([
        jnp.concatenate([p[HALF:, :HALF], q[HALF:, :HALF]], 1),
        jnp.concatenate([p[HALF:, HALF:], q[HALF:, HALF:]], 1)], 0)
    a = left(tab, MET, even)
    b = left(tab, MOT, odd)
    s, d = a + b, a - b
    return jnp.concatenate([s[:HALF], d[:HALF]], 0), jnp.concatenate([s[HALF:], d[HALF:]], 0)


def lanes_left(blocks, shift):
    lane = lax.broadcasted_iota(jnp.int32, blocks[0].shape, 1)
    turned = [pltpu.roll(x, lax.rem(HALF - shift, HALF), 1) for x in blocks]
    keep = lane < HALF - shift
    return [jnp.where(keep, turned[j], turned[j + 1]) for j in range(len(blocks) - 1)]


def lanes_right(blocks, shift):
    lane = lax.broadcasted_iota(jnp.int32, blocks[0].shape, 1)
    turned = [pltpu.roll(x, shift, 1) for x in blocks]
    turned = [jnp.zeros_like(blocks[0])] + turned + [jnp.zeros_like(blocks[0])]
    keep = lane >= shift
    return [jnp.where(keep, turned[j + 1], turned[j]) for j in range(len(blocks) + 1)]


def compute_kernel(top_ref, col_ref, live_ref, obj_hbm, low_hbm, right_hbm, probe_ref, int_ref, tab, perm_ref,
                   gmain_ref, gright_ref, pg_ref, ext, grad, patch, spec, contrib, amp, sems):
    copies = [
        pltpu.make_async_copy(obj_hbm, ext.at[:, pl.ds(0, TILE), pl.ds(0, TILE)], sems.at[0]),
        pltpu.make_async_copy(low_hbm, ext.at[:, pl.ds(TILE, W), pl.ds(0, TILE)], sems.at[1]),
        pltpu.make_async_copy(right_hbm, ext.at[:, :, pl.ds(TILE, W)], sems.at[2]),
    ]
    for c in copies:
        c.start()
    grad[...] = jnp.zeros_like(grad)
    contrib[...] = jnp.zeros_like(contrib)
    amp[...] = jnp.zeros_like(amp)
    for c in copies:
        c.wait()
    for k in range(2):
        t = top_ref[k]
        l = col_ref[k]
        base = pl.multiple_of(l // HALF * HALF, HALF)
        start = pl.multiple_of(t // 8 * 8, 8)
        for c in range(2):
            rows = ext[c, pl.ds(start, W + 8), pl.ds(base, 3 * HALF)]
            rows = pltpu.roll(rows, W + 8 - (t - start), 0)[:W]
            got = lanes_left([rows[:, j * HALF:(j + 1) * HALF] for j in range(3)], l - base)
            patch[k, c] = jnp.concatenate(got, 1)

    def forward(m, carry):
        pr, pi = probe_ref[0, m], probe_ref[1, m]
        for k in range(2):
            o_r, o_i = patch[k, 0], patch[k, 1]
            fe, fo = transform(pr * o_r - pi * o_i, pr * o_i + pi * o_r, tab)
            spec[k, m, 0] = fe
            spec[k, m, 1] = fo
            fe2, fo2 = fe * fe, fo * fo
            amp[k] += jnp.concatenate([fe2[:, :HALF] + fe2[:, HALF:], fo2[:, :HALF] + fo2[:, HALF:]], 1)
        return carry

    lax.fori_loop(0, MODES, forward, 0)

    for k in range(2):
        hi, lo = parts(jnp.sqrt(int_ref[k]))
        hi, lo = dot(perm_ref[1], hi).astype(BF), dot(perm_ref[1], lo).astype(BF)
        root = dot(hi, perm_ref[0]) + dot(lo, perm_ref[0])
        alive = live_ref[k].astype(F32)
        amp[k] = (1.0 - root / jnp.sqrt(amp[k] + 0.25)) * alive

    def backward(m, carry):
        pr, pi = probe_ref[0, m], probe_ref[1, m]
        gr = gi = None
        for k in range(2):
            o_r, o_i = patch[k, 0], patch[k, 1]
            f = amp[k]
            fe, fo = f[:, :HALF], f[:, HALF:]
            chi_r, chi_i = inverse(spec[k, m, 0] * jnp.concatenate([fe, fe], 1), spec[k, m, 1] * jnp.concatenate([fo, fo], 1), tab)
            contrib[k, 0] += pr * chi_r + pi * chi_i
            contrib[k, 1] += pr * chi_i - pi * chi_r
            qr = o_r * chi_r + o_i * chi_i
            qi = o_r * chi_i - o_i * chi_r
            gr = qr if gr is None else gr + qr
            gi = qi if gi is None else gi + qi
        pg_ref[0, m] = gr
        pg_ref[1, m] = gi
        return carry

    lax.fori_loop(0, MODES, backward, 0)

    for k in range(2):
        t = top_ref[k]
        l = col_ref[k]
        base = pl.multiple_of(l // HALF * HALF, HALF)
        start = pl.multiple_of(t // 8 * 8, 8)
        for c in range(2):
            g = contrib[k, c]
            wide = jnp.concatenate(lanes_right([g[:, :HALF], g[:, HALF:]], l - base), 1)
            wide = pltpu.roll(jnp.concatenate([wide, jnp.zeros((8, 3 * HALF), F32)], 0), t - start, 0)
            grad[c, pl.ds(start, W + 8), pl.ds(base, 3 * HALF)] += wide
    out = [
        pltpu.make_async_copy(grad.at[:, :, pl.ds(0, TILE)], gmain_ref, sems.at[0]),
        pltpu.make_async_copy(grad.at[:, :, pl.ds(TILE, W)], gright_ref, sems.at[1]),
    ]
    for c in out:
        c.start()
    for c in out:
        c.wait()


def compute(top, col, live, obj, low, rgt, probe, intensity):
    tab = jnp.asarray(tables())
    perm = jnp.asarray(column_order())
    smem = pl.BlockSpec(memory_space=pltpu.SMEM)
    vmem = pl.BlockSpec(memory_space=pltpu.VMEM)
    hbm = pl.BlockSpec(memory_space=pl.ANY)
    return pl.pallas_call(
        compute_kernel,
        out_shape=(
            jax.ShapeDtypeStruct((2, EXT, TILE), F32),
            jax.ShapeDtypeStruct((2, EXT, W), F32),
            jax.ShapeDtypeStruct((2, MODES, W, W), F32),
        ),
        in_specs=[smem, smem, smem, hbm, hbm, hbm, vmem, vmem, vmem, vmem],
        out_specs=(hbm, hbm, vmem),
        scratch_shapes=[
            pltpu.VMEM((2, EXT, EXT), F32),
            pltpu.VMEM((2, EXT, EXT), F32),
            pltpu.VMEM((2, 2, W, W), F32),
            pltpu.VMEM((2, MODES, 2, W, W), F32),
            pltpu.VMEM((2, 2, W, W), F32),
            pltpu.VMEM((2, W, W), F32),
            pltpu.SemaphoreType.DMA((3,)),
        ],
        compiler_params=pltpu.CompilerParams(vmem_limit_bytes=60 * 1024 * 1024),
        name="ptycho",
    )(top, col, live, obj, low, rgt, probe, intensity, tab, perm)


MESH = pl.DeviceIdType.MESH
N_ROW, N_COL = 8, 16


def place():
    row, col = lax.axis_index("row"), lax.axis_index("col")
    return row, col


def remote(src, dst, send, recv, to):
    return pltpu.make_async_remote_copy(src_ref=src, dst_ref=dst, send_sem=send, recv_sem=recv, device_id=to, device_id_type=MESH)


def count(flags):
    return sum(f.astype(jnp.int32) for f in flags)


def gather_kernel(obj, low, rgt, zero, send, recv, zsem):
    row, col = place()
    up, down, lft, rht = row > 0, row < N_ROW - 1, col > 0, col < N_COL - 1
    barrier = pltpu.get_barrier_semaphore()
    for ok, dev in ((up, (row - 1, col)), (down, (row + 1, col)), (lft, (row, col - 1)), (rht, (row, col + 1))):
        @pl.when(ok)
        def _():
            pl.semaphore_signal(barrier, inc=1, device_id=dev, device_id_type=MESH)
    pl.semaphore_wait(barrier, count((up, down, lft, rht)))
    above, left = (lax.max(row - 1, 0), col), (row, lax.max(col - 1, 0))
    first = remote(obj.at[:, pl.ds(0, W), pl.ds(0, W)], low.at[:, :, pl.ds(0, W)], send.at[0], recv.at[0], above)
    second = remote(obj.at[:, pl.ds(0, W), pl.ds(W, W)], low.at[:, :, pl.ds(W, W)], send.at[1], recv.at[1], above)
    side = remote(obj.at[:, :, pl.ds(0, W)], rgt.at[:, pl.ds(0, TILE), :], send.at[2], recv.at[2], left)
    corner = remote(low.at[:, :, pl.ds(0, W)], rgt.at[:, pl.ds(TILE, W), :], send.at[3], recv.at[3], left)

    @pl.when(up)
    def _():
        first.start()
        second.start()

    @pl.when(lft)
    def _():
        side.start()

    edge = jnp.logical_not(jnp.logical_and(down, rht))

    @pl.when(edge)
    def _():
        zero[...] = jnp.zeros_like(zero)

    @pl.when(jnp.logical_not(down))
    def _():
        for j in range(2):
            pltpu.make_async_copy(zero, low.at[:, :, pl.ds(j * W, W)], zsem.at[j]).start()
        for j in range(2):
            pltpu.make_async_copy(zero, low.at[:, :, pl.ds(j * W, W)], zsem.at[j]).wait()

    @pl.when(jnp.logical_not(rht))
    def _():
        for j in range(3):
            pltpu.make_async_copy(zero, rgt.at[:, pl.ds(j * W, W), :], zsem.at[j]).start()
        for j in range(3):
            pltpu.make_async_copy(zero, rgt.at[:, pl.ds(j * W, W), :], zsem.at[j]).wait()

    @pl.when(down)
    def _():
        first.wait_recv()

    @pl.when(lft)
    def _():
        corner.start()

    @pl.when(down)
    def _():
        second.wait_recv()

    @pl.when(rht)
    def _():
        side.wait_recv()
        corner.wait_recv()

    @pl.when(up)
    def _():
        first.wait_send()
        second.wait_send()

    @pl.when(lft)
    def _():
        side.wait_send()
        corner.wait_send()


def gather(obj):
    hbm = pl.BlockSpec(memory_space=pl.ANY)
    return pl.pallas_call(
        gather_kernel,
        out_shape=(jax.ShapeDtypeStruct((2, W, TILE), F32), jax.ShapeDtypeStruct((2, EXT, W), F32)),
        in_specs=[hbm],
        out_specs=(hbm, hbm),
        scratch_shapes=[
            pltpu.VMEM((2, W, W), F32),
            pltpu.SemaphoreType.DMA((4,)),
            pltpu.SemaphoreType.DMA((4,)),
            pltpu.SemaphoreType.DMA((3,)),
        ],
        compiler_params=pltpu.CompilerParams(collective_id=0, has_side_effects=True),
        name="halo_in",
    )(obj)


UNITS = (3, 2, 3, 3, 2, 3)
ROWS = 2 * MODES * W
STREAMS = 6
STEPS = 5


def partners():
    row, col = place()
    z_hi, y = row // 4, row % 4
    z_lo, x, core = col // 8, col // 2 % 4, col % 2
    z = z_hi * 2 + z_lo

    def dev(x, y, z, core):
        return (z // 2 * 4 + y, z % 2 * 8 + x * 2 + core)

    def flip(p):
        return p + 1 - 2 * (p % 2)

    def mirror(p):
        return 3 - p

    def gray(p):
        return (p + 1) // 2 % 2

    bits = [
        (gray(x), dev(flip(x), y, z, core)),
        (gray(y), dev(x, flip(y), z, core)),
        (gray(z), dev(x, y, flip(z), core)),
        (x // 2, dev(mirror(x), y, z, core)),
        (y // 2, dev(x, mirror(y), z, core)),
        (z // 2, dev(x, y, mirror(z), core)),
    ]
    return bits, core, dev(x, y, z, 1 - core)


def reduce_kernel(part, gmain, gright, total, own, data, first, later, gath, tile, add_c, add_r, add_l, asend, arecv, csend, crecv, lsem, osem, hsend, hrecv, gsem):
    row, col = place()
    bits, core, twin = partners()
    up, down, lft, rht = row > 0, row < N_ROW - 1, col > 0, col < N_COL - 1
    barrier = pltpu.get_barrier_semaphore()
    for dev in [twin] + [b[1] for b in bits]:
        pl.semaphore_signal(barrier, inc=1, device_id=dev, device_id_type=MESH)
    for ok, dev in ((up, (row - 1, col)), (down, (row + 1, col)), (lft, (row, col - 1)), (rht, (row, col + 1))):
        @pl.when(ok)
        def _():
            pl.semaphore_signal(barrier, inc=1, device_id=dev, device_id_type=MESH)
    mine = pl.ds(pl.multiple_of(core * HALF, HALF), HALF)
    other = pl.ds(pl.multiple_of((1 - core) * HALF, HALF), HALF)
    base = [sum(UNITS[:s]) * 256 for s in range(STREAMS)]
    size = [u * 256 for u in UNITS]
    loads = [pltpu.make_async_copy(part.at[pl.ds(base[s], size[s]), mine], data.at[pl.ds(base[s], size[s]), :], lsem.at[s]) for s in range(STREAMS)]
    for c in loads:
        c.start()
    halo_loads = [pltpu.make_async_copy(gmain, tile, gsem.at[0])]
    for c in halo_loads:
        c.start()
    pl.semaphore_wait(barrier, 7 + count((up, down, lft, rht)))

    pair = [remote(part.at[pl.ds(base[s], size[s]), other], first.at[pl.ds(base[s], size[s]), :], asend.at[0, s], arecv.at[0, s], twin) for s in range(STREAMS)]
    for c in pair:
        c.start()

    below, right = (lax.min(row + 1, N_ROW - 1), col), (row, lax.min(col + 1, N_COL - 1))
    h_corner = remote(gright.at[:, pl.ds(TILE, W), :], add_c, hsend.at[0], hrecv.at[0], right)
    h_low1 = remote(gmain.at[:, pl.ds(TILE, W), pl.ds(W, W)], add_l.at[:, :, pl.ds(W, W)], hsend.at[1], hrecv.at[1], below)
    h_right = remote(gright.at[:, pl.ds(0, TILE), :], add_r, hsend.at[2], hrecv.at[2], right)
    h_low0 = remote(tile.at[:, pl.ds(TILE, W), pl.ds(0, W)], add_l.at[:, :, pl.ds(0, W)], hsend.at[3], hrecv.at[3], below)

    @pl.when(rht)
    def _():
        h_corner.start()
        h_right.start()

    @pl.when(down)
    def _():
        h_low1.start()

    def start_step(i, s, off):
        g, to = bits[(s + i) % STREAMS]
        n = size[s] >> (i + 1)
        send_off = pl.multiple_of(off + (1 - g) * n, 8)
        keep = pl.multiple_of(off + g * n, 8)
        spot = base[s] + size[s] - (size[s] >> i)
        c = remote(data.at[pl.ds(send_off, n), :], later.at[pl.ds(spot, n), :], asend.at[1 + i, s], arecv.at[1 + i, s], to)
        c.start()
        return c, keep, n, spot

    offs = []
    flights = []
    for s in range(STREAMS):
        loads[s].wait()
        pair[s].wait_recv()
        sl = pl.ds(base[s], size[s])
        data[sl, :] += first[sl, :]
        flights.append(start_step(0, s, base[s]))
        offs.append([base[s]])
    halo_loads[0].wait()

    @pl.when(lft)
    def _():
        h_corner.wait_recv()
        tile[:, pl.ds(TILE, W), pl.ds(0, W)] += add_c[...]

    @pl.when(down)
    def _():
        h_low0.start()

    sends = list(pair)
    for i in range(STEPS):
        for s in range(STREAMS):
            c, keep, n, spot = flights[s]
            c.wait_recv()
            sends.append(c)
            data[pl.ds(keep, n), :] += later[pl.ds(spot, n), :]
            offs[s].append(keep)
            if i + 1 < STEPS:
                flights[s] = start_step(i + 1, s, keep)
            else:
                g, to = bits[(s + STEPS) % STREAMS]
                spot = base[s] + size[s] - n
                c = remote(data.at[pl.ds(keep, n), :], later.at[pl.ds(spot, n), :], asend.at[1 + STEPS, s], arecv.at[1 + STEPS, s], to)
                c.start()
                flights[s] = (c, keep, n, spot)
    gather_step = []
    for s in range(STREAMS):
        c, keep, n, spot = flights[s]
        c.wait()
        gath[pl.ds(keep, n), :] = data[pl.ds(keep, n), :] + later[pl.ds(spot, n), :]
        to = bits[(s + STEPS - 1) % STREAMS][1]
        here = gath.at[pl.ds(keep, n), :]
        d = remote(here, here, csend.at[STEPS - 1, s], crecv.at[STEPS - 1, s], to)
        d.start()
        gather_step.append(d)
    for c in sends:
        c.wait_send()
    last = []
    for i in range(STEPS - 1, -1, -1):
        for s in range(STREAMS):
            gather_step[s].wait()
            if i > 0:
                here = gath.at[pl.ds(offs[s][i], size[s] >> i), :]
                to = bits[(s + i - 1) % STREAMS][1]
                d = remote(here, here, csend.at[i - 1, s], crecv.at[i - 1, s], to)
                d.start()
                gather_step[s] = d
            else:
                sl = pl.ds(base[s], size[s])
                d = remote(gath.at[sl, :], total.at[sl, mine], csend.at[STEPS, s], crecv.at[STEPS, s], twin)
                d.start()
                e = pltpu.make_async_copy(gath.at[sl, :], total.at[sl, mine], osem.at[s])
                e.start()
                last += [d, e]

    @pl.when(lft)
    def _():
        h_right.wait_recv()
        tile[:, pl.ds(0, TILE), pl.ds(0, W)] += add_r[...]

    @pl.when(up)
    def _():
        h_low1.wait_recv()
        h_low0.wait_recv()
        tile[:, pl.ds(0, W), :] += add_l[...]

    result = pltpu.make_async_copy(tile.at[:, pl.ds(0, TILE), :], own, gsem.at[1])
    result.start()

    @pl.when(rht)
    def _():
        h_corner.wait_send()
        h_right.wait_send()

    @pl.when(down)
    def _():
        h_low1.wait_send()
        h_low0.wait_send()

    for d in last:
        d.wait()
    result.wait()


def reduce(part, gmain, gright):
    hbm = pl.BlockSpec(memory_space=pl.ANY)
    dma = pltpu.SemaphoreType.DMA
    return pl.pallas_call(
        reduce_kernel,
        out_shape=(jax.ShapeDtypeStruct((ROWS, W), F32), jax.ShapeDtypeStruct((2, TILE, TILE), F32)),
        in_specs=[hbm] * 3,
        out_specs=(hbm, hbm),
        scratch_shapes=[
            pltpu.VMEM((ROWS, HALF), F32),
            pltpu.VMEM((ROWS, HALF), F32),
            pltpu.VMEM((ROWS, HALF), F32),
            pltpu.VMEM((ROWS, HALF), F32),
            pltpu.VMEM((2, EXT, TILE), F32),
            pltpu.VMEM((2, W, W), F32),
            pltpu.VMEM((2, TILE, W), F32),
            pltpu.VMEM((2, W, TILE), F32),
            dma((2 + STEPS, STREAMS)),
            dma((2 + STEPS, STREAMS)),
            dma((1 + STEPS, STREAMS)),
            dma((1 + STEPS, STREAMS)),
            dma((STREAMS,)),
            dma((STREAMS,)),
            dma((4,)),
            dma((4,)),
            dma((2,)),
        ],
        compiler_params=pltpu.CompilerParams(collective_id=1, has_side_effects=True, vmem_limit_bytes=40 * 1024 * 1024),
        name="reduce_out",
    )(part, gmain, gright)


def shards(object_field, probe, intensity, row_offset, col_offset, live):
    low, rgt = gather(object_field)
    gmain, gright, partial_probe = compute(row_offset, col_offset, live, object_field, low, rgt, probe, intensity)
    total, object_grad = reduce(partial_probe.reshape(ROWS, W), gmain, gright)
    return (object_grad, total.reshape(2, MODES, W, W))


def solution(mesh):
    in_specs = (
        P(None, "row", "col"),
        P(),
        P(("row", "col"), None, None),
        P(("row", "col")),
        P(("row", "col")),
        P(("row", "col")),
    )
    out_specs = (P(None, "row", "col"), P())
    return jax.shard_map(shards, mesh=mesh, in_specs=in_specs, out_specs=out_specs, check_vma=False)
```

```python
import functools
import jax
import jax.numpy as jnp
import numpy as np
from jax import lax
from jax.experimental import pallas as pl
from jax.experimental.pallas import tpu as pltpu
from jax.sharding import PartitionSpec as P

BF = jnp.bfloat16
F32 = jnp.float32
W, MODES, TILE, EXT, HALF = 256, 8, 512, 768, 128


def split_np(m):
    hi = m.astype(np.float32).astype(jnp.bfloat16)
    lo = (m - hi.astype(np.float64)).astype(np.float32).astype(jnp.bfloat16)
    return hi, lo


def tables():
    n = np.arange(HALF)
    out = []
    for odd in (0, 1):
        k = 2 * np.arange(HALF) + odd
        phase = 2.0 * np.pi * ((k[:, None] * n[None, :]) % W) / W
        c, s = np.cos(phase) / 16.0, np.sin(phase) / 16.0
        m = np.block([[c, s], [-s, c]])
        for t in (m, m.T):
            out.extend(split_np(t))
    return np.stack(out)


def column_order():
    q = np.zeros((W, W), np.float32)
    for j in range(HALF):
        q[2 * j, j] = 1.0
        q[2 * j + 1, HALF + j] = 1.0
    return np.stack([q, q.T]).astype(jnp.bfloat16)


def parts(x):
    hi = x.astype(BF)
    lo = (x - hi.astype(F32)).astype(BF)
    return hi, lo


def dot(a, b):
    return jnp.dot(a, b, preferred_element_type=F32)


def left(tab, i, data):
    hi, lo = parts(data)
    return dot(tab[i], hi) + dot(tab[i + 1], hi) + dot(tab[i], lo)


def right(data, tab, i):
    hi, lo = parts(data)
    return dot(hi, tab[i]) + dot(hi, tab[i + 1]) + dot(lo, tab[i])


ME, MET, MO, MOT = 0, 2, 4, 6


def transform(re, im, tab):
    even = jnp.concatenate([re[:HALF] + re[HALF:], im[:HALF] + im[HALF:]], 0)
    odd = jnp.concatenate([re[:HALF] - re[HALF:], im[:HALF] - im[HALF:]], 0)
    ye = left(tab, ME, even)
    yo = left(tab, MO, odd)
    a = jnp.concatenate([
        jnp.concatenate([y[:HALF, :HALF] + y[:HALF, HALF:], y[HALF:, :HALF] + y[HALF:, HALF:]], 1) for y in (ye, yo)], 0)
    b = jnp.concatenate([
        jnp.concatenate([y[:HALF, :HALF] - y[:HALF, HALF:], y[HALF:, :HALF] - y[HALF:, HALF:]], 1) for y in (ye, yo)], 0)
    return right(a, tab, MET), right(b, tab, MOT)


def inverse(fe, fo, tab):
    ge = right(fe, tab, ME)
    go = right(fo, tab, MO)
    p, q = ge + go, ge - go
    even = jnp.concatenate([
        jnp.concatenate([p[:HALF, :HALF], q[:HALF, :HALF]], 1),
        jnp.concatenate([p[:HALF, HALF:], q[:HALF, HALF:]], 1)], 0)
    odd = jnp.concatenate([
        jnp.concatenate([p[HALF:, :HALF], q[HALF:, :HALF]], 1),
        jnp.concatenate([p[HALF:, HALF:], q[HALF:, HALF:]], 1)], 0)
    a = left(tab, MET, even)
    b = left(tab, MOT, odd)
    s, d = a + b, a - b
    return jnp.concatenate([s[:HALF], d[:HALF]], 0), jnp.concatenate([s[HALF:], d[HALF:]], 0)


def picks(shape, axis, offset):
    a, b = lax.broadcasted_iota(jnp.int32, shape, axis), lax.broadcasted_iota(jnp.int32, shape, 1 - axis)
    return jnp.where(a - b == offset, 1.0, 0.0).astype(BF)


def select_left(sel, x):
    hi, lo = parts(x)
    return dot(sel, hi) + dot(sel, lo)


def select_right(x, sel):
    hi, lo = parts(x)
    return dot(hi, sel) + dot(lo, sel)


MESH = pl.DeviceIdType.MESH
N_ROW, N_COL = 8, 16
ROWS = 2 * W
STAGES = 13
RELAY_IN, RELAY_OUT = 1, -1


def remote(src, dst, send, recv, to):
    return pltpu.make_async_remote_copy(src_ref=src, dst_ref=dst, send_sem=send, recv_sem=recv, device_id=to, device_id_type=MESH)


def count(flags):
    return sum(f.astype(jnp.int32) for f in flags)


def both(a, b):
    return jnp.logical_and(a, b)


def hypercube(row, col):
    z_hi, y = row // 4, row % 4
    z_lo, x, core = col // 8, col // 2 % 4, col % 2
    z = z_hi * 2 + z_lo

    def dev(x, y, z):
        return (z // 2 * 4 + y, z % 2 * 8 + x * 2 + core)

    def flip(p):
        return p + 1 - 2 * (p % 2)

    def gray(p):
        return (p + 1) // 2 % 2

    bits = [
        (gray(z),) + dev(x, y, flip(z)),
        (gray(x),) + dev(flip(x), y, z),
        (z // 2,) + dev(x, y, 3 - z),
        (x // 2,) + dev(3 - x, y, z),
    ]
    return bits, core, (row, col + 1 - 2 * core), y, dev(x, (y + 3) % 4, z), dev(x, (y + 1) % 4, z)


def relay_roles(row, col, source, step):
    odd, z_lo = col % 2 == 1, col // 8
    target = 7 - source
    y = source % 4
    first = (source // 4 * 2 + step) % 4
    second = (source // 4 * 2 + 1 + step) % 4
    relay_row = (first // 2 * 4 + y) * (1 - z_lo) + (second // 2 * 4 + y) * z_lo
    is_relay = both(odd, jnp.logical_or(both(row == first // 2 * 4 + y, z_lo == 1), both(row == second // 2 * 4 + y, z_lo == 0)))
    return both(row == source, odd), both(row == target, odd), is_relay, relay_row


def main_kernel(top_ref, col_ref, live_ref, obj, probe_hbm, int_hbm, tab_hbm, perm_hbm, own, total,
                ext, grad, mid, rows_of, cols_of, rows_to, cols_to, patch, spec, contrib, amp, probe, inten, tab, perm, pgm, first, data, later, gath, ring,
                hold_in, hold_out, add_c, add_r, add_l,
                lsem, asend, arecv, osem, isend, irecv, rsend, rrecv, hsend, hrecv, qsend, qrecv):
    row, col = lax.axis_index("row"), lax.axis_index("col")
    bits, core, twin, y, y_next, y_prev = hypercube(row, col)
    up, down, lft, rht = row > 0, row < N_ROW - 1, col > 0, col < N_COL - 1
    in_src, in_dst, in_relay, in_row = relay_roles(row, col, 4, RELAY_IN)
    out_src, out_dst, out_relay, out_row = relay_roles(row, col, 3, RELAY_OUT)
    swap = col + 8 - 16 * (col // 8)
    yes = row >= 0
    no_down, no_rht = jnp.logical_not(down), jnp.logical_not(rht)
    above, below = (lax.max(row - 1, 0), col), (lax.min(row + 1, N_ROW - 1), col)
    left, right = (row, lax.max(col - 1, 0)), (row, lax.min(col + 1, N_COL - 1))

    barrier = pltpu.get_barrier_semaphore()
    peers = [(up, above), (down, below), (lft, left), (rht, right), (yes, twin), (yes, y_next), (yes, y_prev)] + [(yes, b[1:]) for b in bits]
    peers += [(in_src, (in_row, swap)), (in_dst, (in_row, swap)), (in_relay, (4, swap)), (in_relay, (3, swap))]
    peers += [(out_src, (out_row, swap)), (out_dst, (out_row, swap)), (out_relay, (3, swap)), (out_relay, (4, swap))]
    for ok, dev in peers:
        @pl.when(ok)
        def _():
            pl.semaphore_signal(barrier, inc=1, device_id=dev, device_id_type=MESH)

    loads = [
        pltpu.make_async_copy(obj, ext.at[:, pl.ds(0, TILE), pl.ds(0, TILE)], lsem.at[0]),
        pltpu.make_async_copy(probe_hbm, probe, lsem.at[1]),
        pltpu.make_async_copy(tab_hbm, tab, lsem.at[2]),
        pltpu.make_async_copy(int_hbm, inten, lsem.at[3]),
        pltpu.make_async_copy(perm_hbm, perm, lsem.at[4]),
    ]
    pl.semaphore_wait(barrier, count([p[0] for p in peers]))

    pieces = [(c, j) for j in range(2) for c in range(2)]

    def cut(ref, i, start):
        c, j = pieces[i]
        return ref.at[c, pl.ds(start, W), pl.ds(j * W, W)]

    in_direct = [remote(cut(obj, i, 0), cut(ext, i, TILE), isend.at[i], irecv.at[i], above) for i in range(4)]
    in_hop = [remote(cut(obj, i, 0), cut(hold_in, i, 0), rsend.at[i], rrecv.at[i], (in_row, swap)) for i in range(4)]
    in_on = [remote(cut(hold_in, i, 0), cut(ext, i, TILE), rsend.at[4 + i], irecv.at[i], (3, swap)) for i in range(4)]
    side = remote(obj.at[:, :, pl.ds(0, W)], ext.at[:, pl.ds(0, TILE), pl.ds(TILE, W)], isend.at[4], irecv.at[4], left)
    corner = remote(ext.at[:, pl.ds(TILE, W), pl.ds(0, W)], ext.at[:, pl.ds(TILE, W), pl.ds(TILE, W)], isend.at[5], irecv.at[5], left)
    in_up = both(up, jnp.logical_not(in_src))

    @pl.when(in_src)
    def _():
        for c in in_hop:
            c.start()

    @pl.when(in_up)
    def _():
        for c in in_direct:
            c.start()

    @pl.when(lft)
    def _():
        side.start()

    for c in loads:
        c.start()

    @pl.when(no_down)
    def _():
        ext[:, pl.ds(TILE, W), :] = jnp.zeros((2, W, EXT), F32)

    @pl.when(no_rht)
    def _():
        ext[:, pl.ds(0, TILE), pl.ds(TILE, W)] = jnp.zeros((2, TILE, W), F32)
        ext[:, pl.ds(TILE, W), pl.ds(TILE, W)] = jnp.zeros((2, W, W), F32)

    for k in range(2):
        rows_of[pl.ds(k * W, W), :] = picks((W, EXT), 1, top_ref[k])
        cols_of[k] = picks((EXT, W), 0, col_ref[k])
        rows_to[:, pl.ds(k * W, W)] = picks((EXT, W), 0, top_ref[k])
        cols_to[k] = picks((W, EXT), 1, col_ref[k])
    contrib[...] = jnp.zeros_like(contrib)
    amp[...] = jnp.zeros_like(amp)
    for c in loads:
        c.wait()
    for k in range(2):
        hi, lo = parts(jnp.sqrt(inten[k]))
        hi, lo = dot(perm[1], hi).astype(BF), dot(perm[1], lo).astype(BF)
        inten[k] = dot(hi, perm[0]) + dot(lo, perm[0])

    def rows_own(j):
        for c in range(2):
            cols = pl.ds(j * W, W)
            mid[c, :, cols] = select_left(rows_of[:, :TILE], ext[c, pl.ds(0, TILE), cols])

    rows_own(0)
    rows_own(1)

    @pl.when(in_relay)
    def _():
        for i in range(4):
            in_hop[i].wait_recv()
            in_on[i].start()

    @pl.when(down)
    def _():
        in_direct[0].wait_recv()
        in_direct[1].wait_recv()

    @pl.when(both(down, lft))
    def _():
        corner.start()

    @pl.when(rht)
    def _():
        side.wait_recv()

    rows_own(2)

    @pl.when(down)
    def _():
        in_direct[2].wait_recv()
        in_direct[3].wait_recv()

    @pl.when(both(down, rht))
    def _():
        corner.wait_recv()

    for c in range(2):
        for j in range(3):
            cols = pl.ds(j * W, W)
            mid[c, :, cols] += select_left(rows_of[:, TILE:], ext[c, pl.ds(TILE, W), cols])
        for k in range(2):
            patch[k, c] = select_right(mid[c, pl.ds(k * W, W), :], cols_of[k])

    def forward(m, carry):
        pr, pi = probe[0, m], probe[1, m]
        for k in range(2):
            o_r, o_i = patch[k, 0], patch[k, 1]
            fe, fo = transform(pr * o_r - pi * o_i, pr * o_i + pi * o_r, tab)
            spec[k, m, 0] = fe
            spec[k, m, 1] = fo
            fe2, fo2 = fe * fe, fo * fo
            amp[k] += jnp.concatenate([fe2[:, :HALF] + fe2[:, HALF:], fo2[:, :HALF] + fo2[:, HALF:]], 1)
        return carry

    lax.fori_loop(0, MODES, forward, 0)
    for k in range(2):
        alive = live_ref[k].astype(F32)
        amp[k] = (1.0 - inten[k] / jnp.sqrt(amp[k] + 0.25)) * alive

    mine = pl.ds(pl.multiple_of(core * HALF, HALF), HALF)
    other = pl.ds(pl.multiple_of((1 - core) * HALF, HALF), HALF)

    def backward(m):
        pr, pi = probe[0, m], probe[1, m]
        gr = gi = None
        for k in range(2):
            o_r, o_i = patch[k, 0], patch[k, 1]
            f = amp[k]
            fe, fo = f[:, :HALF], f[:, HALF:]
            chi_r, chi_i = inverse(spec[k, m, 0] * jnp.concatenate([fe, fe], 1), spec[k, m, 1] * jnp.concatenate([fo, fo], 1), tab)
            contrib[k, 0] += pr * chi_r + pi * chi_i
            contrib[k, 1] += pr * chi_i - pi * chi_r
            qr = o_r * chi_r + o_i * chi_i
            qi = o_r * chi_i - o_i * chi_r
            gr = qr if gr is None else gr + qr
            gi = qi if gi is None else gi + qi
        pgm[m, pl.ds(0, W), :] = gr
        pgm[m, pl.ds(W, W), :] = gi

    def swap_copy(s):
        return remote(pgm.at[s, :, other], first.at[s], asend.at[0, s], arecv.at[0, s], twin)

    def halving_copy(i, s, off, to):
        n = ROWS >> (i + 1)
        return remote(data.at[s, pl.ds(pl.multiple_of(off, 8), n), :], later.at[s, pl.ds(ROWS - (ROWS >> i), n), :], asend.at[1 + i, s], arecv.at[1 + i, s], to)

    def merge(s):
        data[s] = pgm[s, :, mine] + first[s]

    def begin(s, bit):
        halving_copy(0, s, (1 - bit[0]) * W, bit[1:]).start()

    def tick(tau, turned):
        backward(tau)

        @pl.when(tau > 0)
        def _():
            swap_copy(tau - 1).wait()
            merge(tau - 1)
            begin(tau - 1, turned[3])

        swap_copy(tau).start()
        return turned[1:] + turned[:1]

    lax.fori_loop(0, MODES, tick, tuple(bits))

    def place(c):
        for k in range(2):
            mid[c, pl.ds(k * W, W), :] = select_right(contrib[k, c], cols_to[k])
        for j in range(3):
            cols = pl.ds(j * W, W)
            grad[c, :, cols] = select_left(rows_to[...], mid[c, :, cols])

    place(0)
    swap_copy(MODES - 1).wait()
    merge(MODES - 1)
    begin(MODES - 1, bits[(MODES - 1) % 4])
    place(1)

    h_corner = [remote(grad.at[c, pl.ds(TILE, W), pl.ds(TILE, W)], add_c.at[c], hsend.at[4 + c], hrecv.at[4 + c], right) for c in range(2)]
    h_side = [remote(grad.at[i // 2, pl.ds(i % 2 * W, W), pl.ds(TILE, W)], add_r.at[i // 2, pl.ds(i % 2 * W, W), :], hsend.at[6 + i], hrecv.at[6 + i], right) for i in range(4)]
    h_direct = [remote(cut(grad, i, TILE), cut(add_l, i, 0), hsend.at[i], hrecv.at[i], below) for i in range(4)]
    h_hop = [remote(cut(grad, i, TILE), cut(hold_out, i, 0), qsend.at[i], qrecv.at[i], (out_row, swap)) for i in range(4)]
    h_on = [remote(cut(hold_out, i, 0), cut(add_l, i, 0), qsend.at[4 + i], hrecv.at[i], (4, swap)) for i in range(4)]
    out_down = both(down, jnp.logical_not(out_src))

    def send_down(i):
        @pl.when(out_src)
        def _():
            h_hop[i].start()

        @pl.when(out_down)
        def _():
            h_direct[i].start()

    def send_side(*which):
        @pl.when(rht)
        def _():
            for i in which:
                h_side[i].start()

    def pass_on(*which):
        @pl.when(out_relay)
        def _():
            for i in which:
                h_hop[i].wait_recv()
                h_on[i].start()

    def turn_corner(c):
        @pl.when(both(down, lft))
        def _():
            h_corner[c].wait_recv()
            grad[c, pl.ds(TILE, W), pl.ds(0, W)] += add_c[c]

        send_down(c)

    @pl.when(both(down, rht))
    def _():
        h_corner[0].start()
        h_corner[1].start()

    send_down(2)
    send_down(3)

    offs = [[bits[s % 4][0] * W] for s in range(MODES)]
    flying = [halving_copy(0, s, (1 - bits[s % 4][0]) * W, bits[s % 4][1:]) for s in range(MODES)]

    def halve(i):
        for s in range(MODES):
            n = ROWS >> i
            off = offs[s][-1]
            flying[s].wait()
            data[s, pl.ds(pl.multiple_of(off, 8), n), :] += later[s, pl.ds(ROWS - (ROWS >> (i - 1)), n), :]
            if i < 4:
                g, to = bits[(s + i) % 4][0], bits[(s + i) % 4][1:]
                flying[s] = halving_copy(i, s, off + (1 - g) * (n // 2), to)
                flying[s].start()
                offs[s].append(off + g * (n // 2))
            else:
                ring[3, s] = data[s, pl.ds(pl.multiple_of(off, 8), n), :]
                flying[s] = remote(ring.at[3, s], ring.at[0, s], asend.at[5, s], arecv.at[5, s], y_next)
                flying[s].start()

    def around(i):
        for s in range(MODES):
            flying[s].wait()
            flying[s] = remote(ring.at[i - 1, s], ring.at[i, s], asend.at[5 + i, s], arecv.at[5 + i, s], y_next)
            flying[s].start()

    def widen(i):
        n = ROWS >> (i + 1)
        for s in range(MODES):
            flying[s].wait()
            off = pl.multiple_of(offs[s][i], 8)
            if i == 3:
                gath[s, pl.ds(off, n), :] = ((ring[(3 - y) % 4, s] + ring[(4 - y) % 4, s]) + (ring[(5 - y) % 4, s] + ring[(6 - y) % 4, s]))
            here = gath.at[s, pl.ds(off, n), :]
            flying[s] = remote(here, here, asend.at[11 - i, s], arecv.at[11 - i, s], bits[(s + i) % 4][1:])
            flying[s].start()

    halve(1)
    halve(2)
    pass_on(2)
    halve(3)
    turn_corner(0)
    pass_on(3)
    halve(4)
    send_side(0, 1)
    turn_corner(1)
    around(1)
    send_side(2)
    around(2)
    send_side(3)
    widen(3)
    pass_on(0)
    widen(2)
    pass_on(1)
    widen(1)
    widen(0)
    last = []
    for s in range(MODES):
        flying[s].wait()
        for c in range(2):
            here, there = gath.at[s, pl.ds(c * W, W), :], total.at[c, s, :, mine]
            last += [remote(here, there, asend.at[12 + c, s], arecv.at[12 + c, s], twin), pltpu.make_async_copy(here, there, osem.at[c, s])]
            last[-2].start()
            last[-1].start()

    @pl.when(lft)
    def _():
        for i in range(4):
            h_side[i].wait_recv()
        grad[:, pl.ds(0, TILE), pl.ds(0, W)] += add_r[...]

    @pl.when(up)
    def _():
        for c in h_direct:
            c.wait_recv()
        grad[:, pl.ds(0, W), pl.ds(0, TILE)] += add_l[...]

    result = pltpu.make_async_copy(grad.at[:, pl.ds(0, TILE), pl.ds(0, TILE)], own, lsem.at[0])
    result.start()

    @pl.when(in_src)
    def _():
        for c in in_hop:
            c.wait_send()

    @pl.when(in_up)
    def _():
        for c in in_direct:
            c.wait_send()

    @pl.when(in_relay)
    def _():
        for c in in_on:
            c.wait_send()

    @pl.when(lft)
    def _():
        side.wait_send()

    @pl.when(both(down, lft))
    def _():
        corner.wait_send()

    @pl.when(both(down, rht))
    def _():
        for c in h_corner:
            c.wait_send()

    @pl.when(rht)
    def _():
        for c in h_side:
            c.wait_send()

    @pl.when(out_src)
    def _():
        for c in h_hop:
            c.wait_send()

    @pl.when(out_down)
    def _():
        for c in h_direct:
            c.wait_send()

    @pl.when(out_relay)
    def _():
        for c in h_on:
            c.wait_send()

    for c in last:
        c.wait()
    result.wait()


def shards(object_field, probe, intensity, row_offset, col_offset, live):
    smem = pl.BlockSpec(memory_space=pltpu.SMEM)
    hbm = pl.BlockSpec(memory_space=pl.ANY)
    dma = pltpu.SemaphoreType.DMA
    half = pltpu.VMEM((MODES, ROWS, HALF), F32)
    object_grad, probe_grad = pl.pallas_call(
        main_kernel,
        out_shape=(
            jax.ShapeDtypeStruct((2, TILE, TILE), F32),
            jax.ShapeDtypeStruct((2, MODES, W, W), F32),
        ),
        in_specs=[smem, smem, smem, hbm, hbm, hbm, hbm, hbm],
        out_specs=(hbm, hbm),
        scratch_shapes=[
            pltpu.VMEM((2, EXT, EXT), F32),
            pltpu.VMEM((2, EXT, EXT), F32),
            pltpu.VMEM((2, 2 * W, EXT), F32),
            pltpu.VMEM((2 * W, EXT), BF),
            pltpu.VMEM((2, EXT, W), BF),
            pltpu.VMEM((EXT, 2 * W), BF),
            pltpu.VMEM((2, W, EXT), BF),
            pltpu.VMEM((2, 2, W, W), F32),
            pltpu.VMEM((2, MODES, 2, W, W), F32),
            pltpu.VMEM((2, 2, W, W), F32),
            pltpu.VMEM((2, W, W), F32),
            pltpu.VMEM((2, MODES, W, W), F32),
            pltpu.VMEM((2, W, W), F32),
            pltpu.VMEM((8, W, W), BF),
            pltpu.VMEM((2, W, W), BF),
            pltpu.VMEM((MODES, ROWS, W), F32),
            half, half, half, half,
            pltpu.VMEM((4, MODES, ROWS // 16, HALF), F32),
            pltpu.VMEM((2, W, TILE), F32),
            pltpu.VMEM((2, W, TILE), F32),
            pltpu.VMEM((2, W, W), F32),
            pltpu.VMEM((2, TILE, W), F32),
            pltpu.VMEM((2, W, TILE), F32),
            dma((5,)), dma((STAGES + 1, MODES)), dma((STAGES + 1, MODES)), dma((2, MODES)),
            dma((6,)), dma((6,)), dma((8,)), dma((4,)), dma((10,)), dma((10,)), dma((8,)), dma((4,)),
        ],
        compiler_params=pltpu.CompilerParams(collective_id=0, has_side_effects=True, vmem_limit_bytes=62 * 1024 * 1024),
        name="ptycho",
    )(row_offset, col_offset, live, object_field, probe, intensity, jnp.asarray(tables()), jnp.asarray(column_order()))
    return (object_grad, probe_grad)


def solution(mesh):
    in_specs = (
        P(None, "row", "col"),
        P(),
        P(("row", "col"), None, None),
        P(("row", "col")),
        P(("row", "col")),
        P(("row", "col")),
    )
    out_specs = (P(None, "row", "col"), P())
    return jax.shard_map(shards, mesh=mesh, in_specs=in_specs, out_specs=out_specs, check_vma=False)
```

```python
import functools
import jax
import jax.numpy as jnp
import numpy as np
from jax import lax
from jax.experimental import pallas as pl
from jax.experimental.pallas import tpu as pltpu
from jax.sharding import PartitionSpec as P

BF = jnp.bfloat16
F32 = jnp.float32
W, MODES, TILE, EXT, HALF = 256, 8, 512, 768, 128


def split_np(m):
    hi = m.astype(np.float32).astype(jnp.bfloat16)
    lo = (m - hi.astype(np.float64)).astype(np.float32).astype(jnp.bfloat16)
    return hi, lo


def tables():
    n = np.arange(HALF)
    out = []
    for odd in (0, 1):
        k = 2 * np.arange(HALF) + odd
        phase = 2.0 * np.pi * ((k[:, None] * n[None, :]) % W) / W
        c, s = np.cos(phase) / 16.0, np.sin(phase) / 16.0
        m = np.block([[c, s], [-s, c]])
        for t in (m, m.T):
            out.extend(split_np(t))
    return np.stack(out)


def column_order():
    q = np.zeros((W, W), np.float32)
    for j in range(HALF):
        q[2 * j, j] = 1.0
        q[2 * j + 1, HALF + j] = 1.0
    return np.stack([q, q.T]).astype(jnp.bfloat16)


def parts(x):
    hi = x.astype(BF)
    lo = (x - hi.astype(F32)).astype(BF)
    return hi, lo


def dot(a, b):
    return jnp.dot(a, b, preferred_element_type=F32)


def left(tab, i, data):
    hi, lo = parts(data)
    return dot(tab[i], hi) + dot(tab[i + 1], hi) + dot(tab[i], lo)


def right(data, tab, i):
    hi, lo = parts(data)
    return dot(hi, tab[i]) + dot(hi, tab[i + 1]) + dot(lo, tab[i])


ME, MET, MO, MOT = 0, 2, 4, 6


def transform(re, im, tab):
    even = jnp.concatenate([re[:HALF] + re[HALF:], im[:HALF] + im[HALF:]], 0)
    odd = jnp.concatenate([re[:HALF] - re[HALF:], im[:HALF] - im[HALF:]], 0)
    ye = left(tab, ME, even)
    yo = left(tab, MO, odd)
    a = jnp.concatenate([
        jnp.concatenate([y[:HALF, :HALF] + y[:HALF, HALF:], y[HALF:, :HALF] + y[HALF:, HALF:]], 1) for y in (ye, yo)], 0)
    b = jnp.concatenate([
        jnp.concatenate([y[:HALF, :HALF] - y[:HALF, HALF:], y[HALF:, :HALF] - y[HALF:, HALF:]], 1) for y in (ye, yo)], 0)
    return right(a, tab, MET), right(b, tab, MOT)


def inverse(fe, fo, tab):
    ge = right(fe, tab, ME)
    go = right(fo, tab, MO)
    p, q = ge + go, ge - go
    even = jnp.concatenate([
        jnp.concatenate([p[:HALF, :HALF], q[:HALF, :HALF]], 1),
        jnp.concatenate([p[:HALF, HALF:], q[:HALF, HALF:]], 1)], 0)
    odd = jnp.concatenate([
        jnp.concatenate([p[HALF:, :HALF], q[HALF:, :HALF]], 1),
        jnp.concatenate([p[HALF:, HALF:], q[HALF:, HALF:]], 1)], 0)
    a = left(tab, MET, even)
    b = left(tab, MOT, odd)
    s, d = a + b, a - b
    return jnp.concatenate([s[:HALF], d[:HALF]], 0), jnp.concatenate([s[HALF:], d[HALF:]], 0)


def picks(shape, axis, offset):
    a, b = lax.broadcasted_iota(jnp.int32, shape, axis), lax.broadcasted_iota(jnp.int32, shape, 1 - axis)
    return jnp.where(a - b == offset, 1.0, 0.0).astype(BF)


def select_left(sel, x):
    hi, lo = parts(x)
    return dot(sel, hi) + dot(sel, lo)


def select_right(x, sel):
    hi, lo = parts(x)
    return dot(hi, sel) + dot(lo, sel)


MESH = pl.DeviceIdType.MESH
N_ROW, N_COL = 8, 16
ROWS = 2 * W
STAGES = 13
OUT_STEPS = (0, -1)


def remote(src, dst, send, recv, to):
    return pltpu.make_async_remote_copy(src_ref=src, dst_ref=dst, send_sem=send, recv_sem=recv, device_id=to, device_id_type=MESH)


def count(flags):
    return sum(f.astype(jnp.int32) for f in flags)


def both(a, b):
    return jnp.logical_and(a, b)


def hypercube(row, col):
    z_hi, y = row // 4, row % 4
    z_lo, x, core = col // 8, col // 2 % 4, col % 2
    z = z_hi * 2 + z_lo

    def dev(x, y, z):
        return (z // 2 * 4 + y, z % 2 * 8 + x * 2 + core)

    def flip(p):
        return p + 1 - 2 * (p % 2)

    def gray(p):
        return (p + 1) // 2 % 2

    bits = [
        (gray(z),) + dev(x, y, flip(z)),
        (gray(x),) + dev(flip(x), y, z),
        (z // 2,) + dev(x, y, 3 - z),
        (x // 2,) + dev(3 - x, y, z),
    ]
    return bits, core, (row, col + 1 - 2 * core), y, dev(x, (y + 3) % 4, z), dev(x, (y + 1) % 4, z)


def relay_roles(row, col, source, step):
    core, z_lo, y = col % 2, col // 8, source % 4
    move = step[0] * (1 - core) + step[1] * core
    first = (source // 4 * 2 + 4 + move) % 4 // 2 * 4 + y
    second = (source // 4 * 2 + 5 + move) % 4 // 2 * 4 + y
    used = move != 0
    is_relay = jnp.logical_or(both(row == first, z_lo == 1), both(row == second, z_lo == 0))
    return both(used, row == source), both(used, row == 7 - source), both(used, is_relay), first * (1 - z_lo) + second * z_lo


def main_kernel(top_ref, col_ref, live_ref, obj, probe_hbm, int_hbm, tab_hbm, perm_hbm, own, total,
                ext, grad, mid, rows_of, cols_of, rows_to, cols_to, patch, spec, contrib, amp, probe, inten, tab, perm, pgm, first, data, later, gath, ring,
                hold_in, hold_out, add_c, add_r, add_l,
                lsem, asend, arecv, osem, isend, irecv, rsend, rrecv, hsend, hrecv, qsend, qrecv):
    row, col = lax.axis_index("row"), lax.axis_index("col")
    bits, core, twin, y, y_next, y_prev = hypercube(row, col)
    up, down, lft, rht = row > 0, row < N_ROW - 1, col > 0, col < N_COL - 1
    in_src, in_dst, in_relay, in_row = relay_roles(row, col, 4, (0, 1))
    out_src, out_dst, out_relay, out_row = relay_roles(row, col, 3, OUT_STEPS)
    swap = col + 8 - 16 * (col // 8)
    yes = row >= 0
    no_down, no_rht = jnp.logical_not(down), jnp.logical_not(rht)
    above, below = (lax.max(row - 1, 0), col), (lax.min(row + 1, N_ROW - 1), col)
    left, right = (row, lax.max(col - 1, 0)), (row, lax.min(col + 1, N_COL - 1))

    barrier = pltpu.get_barrier_semaphore()
    peers = [(up, above), (down, below), (lft, left), (rht, right), (yes, twin), (yes, y_next), (yes, y_prev)] + [(yes, b[1:]) for b in bits]
    peers += [(in_src, (in_row, swap)), (in_dst, (in_row, swap)), (in_relay, (4, swap)), (in_relay, (3, swap))]
    peers += [(out_src, (out_row, swap)), (out_dst, (out_row, swap)), (out_relay, (3, swap)), (out_relay, (4, swap))]
    for ok, dev in peers:
        @pl.when(ok)
        def _():
            pl.semaphore_signal(barrier, inc=1, device_id=dev, device_id_type=MESH)

    loads = [
        pltpu.make_async_copy(obj, ext.at[:, pl.ds(0, TILE), pl.ds(0, TILE)], lsem.at[0]),
        pltpu.make_async_copy(probe_hbm, probe, lsem.at[1]),
        pltpu.make_async_copy(tab_hbm, tab, lsem.at[2]),
        pltpu.make_async_copy(int_hbm, inten, lsem.at[3]),
        pltpu.make_async_copy(perm_hbm, perm, lsem.at[4]),
    ]
    pl.semaphore_wait(barrier, count([p[0] for p in peers]))

    pieces = [(c, j) for j in range(2) for c in range(2)]

    def cut(ref, i, start):
        c, j = pieces[i]
        return ref.at[c, pl.ds(start, W), pl.ds(j * W, W)]

    in_direct = [remote(cut(obj, i, 0), cut(ext, i, TILE), isend.at[i], irecv.at[i], above) for i in range(4)]
    in_hop = [remote(cut(obj, i, 0), cut(hold_in, i, 0), rsend.at[i], rrecv.at[i], (in_row, swap)) for i in range(4)]
    in_on = [remote(cut(hold_in, i, 0), cut(ext, i, TILE), rsend.at[4 + i], irecv.at[i], (3, swap)) for i in range(4)]
    side = remote(obj.at[:, :, pl.ds(0, W)], ext.at[:, pl.ds(0, TILE), pl.ds(TILE, W)], isend.at[4], irecv.at[4], left)
    corner = remote(ext.at[:, pl.ds(TILE, W), pl.ds(0, W)], ext.at[:, pl.ds(TILE, W), pl.ds(TILE, W)], isend.at[5], irecv.at[5], left)
    in_up = both(up, jnp.logical_not(in_src))

    @pl.when(in_src)
    def _():
        for c in in_hop:
            c.start()

    @pl.when(in_up)
    def _():
        for c in in_direct:
            c.start()

    @pl.when(lft)
    def _():
        side.start()

    for c in loads:
        c.start()

    @pl.when(no_down)
    def _():
        ext[:, pl.ds(TILE, W), :] = jnp.zeros((2, W, EXT), F32)

    @pl.when(no_rht)
    def _():
        ext[:, pl.ds(0, TILE), pl.ds(TILE, W)] = jnp.zeros((2, TILE, W), F32)
        ext[:, pl.ds(TILE, W), pl.ds(TILE, W)] = jnp.zeros((2, W, W), F32)

    for k in range(2):
        rows_of[pl.ds(k * W, W), :] = picks((W, EXT), 1, top_ref[k])
        cols_of[k] = picks((EXT, W), 0, col_ref[k])
        rows_to[:, pl.ds(k * W, W)] = picks((EXT, W), 0, top_ref[k])
        cols_to[k] = picks((W, EXT), 1, col_ref[k])
    contrib[...] = jnp.zeros_like(contrib)
    amp[...] = jnp.zeros_like(amp)
    for c in loads:
        c.wait()
    for k in range(2):
        hi, lo = parts(jnp.sqrt(inten[k]))
        hi, lo = dot(perm[1], hi).astype(BF), dot(perm[1], lo).astype(BF)
        inten[k] = dot(hi, perm[0]) + dot(lo, perm[0])

    def rows_own(j):
        for c in range(2):
            cols = pl.ds(j * W, W)
            mid[c, :, cols] = select_left(rows_of[:, :TILE], ext[c, pl.ds(0, TILE), cols])

    rows_own(0)
    rows_own(1)

    @pl.when(in_relay)
    def _():
        for i in range(4):
            in_hop[i].wait_recv()
            in_on[i].start()

    @pl.when(down)
    def _():
        in_direct[0].wait_recv()
        in_direct[1].wait_recv()

    @pl.when(both(down, lft))
    def _():
        corner.start()

    @pl.when(rht)
    def _():
        side.wait_recv()

    rows_own(2)

    @pl.when(down)
    def _():
        in_direct[2].wait_recv()
        in_direct[3].wait_recv()

    @pl.when(both(down, rht))
    def _():
        corner.wait_recv()

    for c in range(2):
        for j in range(3):
            cols = pl.ds(j * W, W)
            mid[c, :, cols] += select_left(rows_of[:, TILE:], ext[c, pl.ds(TILE, W), cols])
        for k in range(2):
            patch[k, c] = select_right(mid[c, pl.ds(k * W, W), :], cols_of[k])

    def forward(m, carry):
        pr, pi = probe[0, m], probe[1, m]
        for k in range(2):
            o_r, o_i = patch[k, 0], patch[k, 1]
            fe, fo = transform(pr * o_r - pi * o_i, pr * o_i + pi * o_r, tab)
            spec[k, m, 0] = fe
            spec[k, m, 1] = fo
            fe2, fo2 = fe * fe, fo * fo
            amp[k] += jnp.concatenate([fe2[:, :HALF] + fe2[:, HALF:], fo2[:, :HALF] + fo2[:, HALF:]], 1)
        return carry

    lax.fori_loop(0, MODES, forward, 0, unroll=2)
    for k in range(2):
        alive = live_ref[k].astype(F32)
        amp[k] = (1.0 - inten[k] / jnp.sqrt(amp[k] + 0.25)) * alive

    mine = pl.ds(pl.multiple_of(core * HALF, HALF), HALF)
    other = pl.ds(pl.multiple_of((1 - core) * HALF, HALF), HALF)

    def backward(m):
        pr, pi = probe[0, m], probe[1, m]
        gr = gi = None
        for k in range(2):
            o_r, o_i = patch[k, 0], patch[k, 1]
            f = amp[k]
            fe, fo = f[:, :HALF], f[:, HALF:]
            chi_r, chi_i = inverse(spec[k, m, 0] * jnp.concatenate([fe, fe], 1), spec[k, m, 1] * jnp.concatenate([fo, fo], 1), tab)
            contrib[k, 0] += pr * chi_r + pi * chi_i
            contrib[k, 1] += pr * chi_i - pi * chi_r
            qr = o_r * chi_r + o_i * chi_i
            qi = o_r * chi_i - o_i * chi_r
            gr = qr if gr is None else gr + qr
            gi = qi if gi is None else gi + qi
        pgm[m, pl.ds(0, W), :] = gr
        pgm[m, pl.ds(W, W), :] = gi

    def swap_copy(s):
        return remote(pgm.at[s, :, other], first.at[s], asend.at[0, s], arecv.at[0, s], twin)

    def halving_copy(i, s, off, to):
        n = ROWS >> (i + 1)
        return remote(data.at[s, pl.ds(pl.multiple_of(off, 8), n), :], later.at[s, pl.ds(ROWS - (ROWS >> i), n), :], asend.at[1 + i, s], arecv.at[1 + i, s], to)

    def merge(s):
        data[s] = pgm[s, :, mine] + first[s]

    def begin(s, bit):
        halving_copy(0, s, (1 - bit[0]) * W, bit[1:]).start()

    def tick(tau, turned):
        backward(tau)

        @pl.when(tau > 0)
        def _():
            swap_copy(tau - 1).wait()
            merge(tau - 1)
            begin(tau - 1, turned[3])

        swap_copy(tau).start()
        return turned[1:] + turned[:1]

    lax.fori_loop(0, MODES, tick, tuple(bits))

    def place(c):
        for k in range(2):
            mid[c, pl.ds(k * W, W), :] = select_right(contrib[k, c], cols_to[k])
        for j in range(3):
            cols = pl.ds(j * W, W)
            grad[c, :, cols] = select_left(rows_to[...], mid[c, :, cols])

    place(0)
    swap_copy(MODES - 1).wait()
    merge(MODES - 1)
    begin(MODES - 1, bits[(MODES - 1) % 4])
    place(1)

    h_corner = [remote(grad.at[c, pl.ds(TILE, W), pl.ds(TILE, W)], add_c.at[c], hsend.at[4 + c], hrecv.at[4 + c], right) for c in range(2)]
    h_side = [remote(grad.at[i // 2, pl.ds(i % 2 * W, W), pl.ds(TILE, W)], add_r.at[i // 2, pl.ds(i % 2 * W, W), :], hsend.at[6 + i], hrecv.at[6 + i], right) for i in range(4)]
    h_direct = [remote(cut(grad, i, TILE), cut(add_l, i, 0), hsend.at[i], hrecv.at[i], below) for i in range(4)]
    h_hop = [remote(cut(grad, i, TILE), cut(hold_out, i, 0), qsend.at[i], qrecv.at[i], (out_row, swap)) for i in range(4)]
    h_on = [remote(cut(hold_out, i, 0), cut(add_l, i, 0), qsend.at[4 + i], hrecv.at[i], (4, swap)) for i in range(4)]
    out_down = both(down, jnp.logical_not(out_src))

    def send_down(i):
        @pl.when(out_src)
        def _():
            h_hop[i].start()

        @pl.when(out_down)
        def _():
            h_direct[i].start()

    def send_side(*which):
        @pl.when(rht)
        def _():
            for i in which:
                h_side[i].start()

    def pass_on(*which):
        @pl.when(out_relay)
        def _():
            for i in which:
                h_hop[i].wait_recv()
                h_on[i].start()

    def turn_corner(c):
        @pl.when(both(down, lft))
        def _():
            h_corner[c].wait_recv()
            grad[c, pl.ds(TILE, W), pl.ds(0, W)] += add_c[c]

        send_down(c)

    def send_corner(c):
        @pl.when(both(down, rht))
        def _():
            h_corner[c].start()

    send_down(2)
    send_down(3)
    send_corner(0)

    offs = [[bits[s % 4][0] * W] for s in range(MODES)]
    flying = [halving_copy(0, s, (1 - bits[s % 4][0]) * W, bits[s % 4][1:]) for s in range(MODES)]

    def halve(i):
        for s in range(MODES):
            n = ROWS >> i
            off = offs[s][-1]
            flying[s].wait()
            data[s, pl.ds(pl.multiple_of(off, 8), n), :] += later[s, pl.ds(ROWS - (ROWS >> (i - 1)), n), :]
            if i < 4:
                g, to = bits[(s + i) % 4][0], bits[(s + i) % 4][1:]
                flying[s] = halving_copy(i, s, off + (1 - g) * (n // 2), to)
                flying[s].start()
                offs[s].append(off + g * (n // 2))
            else:
                ring[3, s] = data[s, pl.ds(pl.multiple_of(off, 8), n), :]
                flying[s] = remote(ring.at[3, s], ring.at[0, s], asend.at[5, s], arecv.at[5, s], y_next)
                flying[s].start()

    def around(i):
        for s in range(MODES):
            flying[s].wait()
            flying[s] = remote(ring.at[i - 1, s], ring.at[i, s], asend.at[5 + i, s], arecv.at[5 + i, s], y_next)
            flying[s].start()

    def widen(i):
        n = ROWS >> (i + 1)
        for s in range(MODES):
            flying[s].wait()
            off = pl.multiple_of(offs[s][i], 8)
            if i == 3:
                gath[s, pl.ds(off, n), :] = ((ring[(3 - y) % 4, s] + ring[(4 - y) % 4, s]) + (ring[(5 - y) % 4, s] + ring[(6 - y) % 4, s]))
            here = gath.at[s, pl.ds(off, n), :]
            flying[s] = remote(here, here, asend.at[11 - i, s], arecv.at[11 - i, s], bits[(s + i) % 4][1:])
            flying[s].start()
            if i == 0:
                hand_over(s, 0)

    last = []

    def hand_over(s, second):
        c = 1 - bits[s % 4][0] if second else bits[s % 4][0]
        here, there = gath.at[s, pl.ds(pl.multiple_of(c * W, W), W), :], total.at[c, s, :, mine]
        pair = [remote(here, there, asend.at[12 + second, s], arecv.at[12 + second, s], twin), pltpu.make_async_copy(here, there, osem.at[second, s])]
        for d in pair:
            d.start()
        last.extend(pair)

    halve(1)
    halve(2)
    send_corner(1)
    halve(3)
    pass_on(2)
    halve(4)
    turn_corner(0)
    send_side(0)
    around(1)
    turn_corner(1)
    pass_on(3)
    send_side(1)
    around(2)
    send_side(2)
    pass_on(0)
    widen(3)
    pass_on(1)
    send_side(3)
    widen(2)
    widen(1)
    widen(0)
    for s in range(MODES):
        flying[s].wait()
        hand_over(s, 1)

    @pl.when(lft)
    def _():
        for i in range(4):
            h_side[i].wait_recv()
        grad[:, pl.ds(0, TILE), pl.ds(0, W)] += add_r[...]

    @pl.when(up)
    def _():
        for c in h_direct:
            c.wait_recv()
        grad[:, pl.ds(0, W), pl.ds(0, TILE)] += add_l[...]

    result = pltpu.make_async_copy(grad.at[:, pl.ds(0, TILE), pl.ds(0, TILE)], own, lsem.at[0])
    result.start()

    @pl.when(in_src)
    def _():
        for c in in_hop:
            c.wait_send()

    @pl.when(in_up)
    def _():
        for c in in_direct:
            c.wait_send()

    @pl.when(in_relay)
    def _():
        for c in in_on:
            c.wait_send()

    @pl.when(lft)
    def _():
        side.wait_send()

    @pl.when(both(down, lft))
    def _():
        corner.wait_send()

    @pl.when(both(down, rht))
    def _():
        for c in h_corner:
            c.wait_send()

    @pl.when(rht)
    def _():
        for c in h_side:
            c.wait_send()

    @pl.when(out_src)
    def _():
        for c in h_hop:
            c.wait_send()

    @pl.when(out_down)
    def _():
        for c in h_direct:
            c.wait_send()

    @pl.when(out_relay)
    def _():
        for c in h_on:
            c.wait_send()

    for c in last:
        c.wait()
    result.wait()


def shards(object_field, probe, intensity, row_offset, col_offset, live):
    smem = pl.BlockSpec(memory_space=pltpu.SMEM)
    hbm = pl.BlockSpec(memory_space=pl.ANY)
    dma = pltpu.SemaphoreType.DMA
    half = pltpu.VMEM((MODES, ROWS, HALF), F32)
    object_grad, probe_grad = pl.pallas_call(
        main_kernel,
        out_shape=(
            jax.ShapeDtypeStruct((2, TILE, TILE), F32),
            jax.ShapeDtypeStruct((2, MODES, W, W), F32),
        ),
        in_specs=[smem, smem, smem, hbm, hbm, hbm, hbm, hbm],
        out_specs=(hbm, hbm),
        scratch_shapes=[
            pltpu.VMEM((2, EXT, EXT), F32),
            pltpu.VMEM((2, EXT, EXT), F32),
            pltpu.VMEM((2, 2 * W, EXT), F32),
            pltpu.VMEM((2 * W, EXT), BF),
            pltpu.VMEM((2, EXT, W), BF),
            pltpu.VMEM((EXT, 2 * W), BF),
            pltpu.VMEM((2, W, EXT), BF),
            pltpu.VMEM((2, 2, W, W), F32),
            pltpu.VMEM((2, MODES, 2, W, W), F32),
            pltpu.VMEM((2, 2, W, W), F32),
            pltpu.VMEM((2, W, W), F32),
            pltpu.VMEM((2, MODES, W, W), F32),
            pltpu.VMEM((2, W, W), F32),
            pltpu.VMEM((8, W, W), BF),
            pltpu.VMEM((2, W, W), BF),
            pltpu.VMEM((MODES, ROWS, W), F32),
            half, half, half, half,
            pltpu.VMEM((4, MODES, ROWS // 16, HALF), F32),
            pltpu.VMEM((2, W, TILE), F32),
            pltpu.VMEM((2, W, TILE), F32),
            pltpu.VMEM((2, W, W), F32),
            pltpu.VMEM((2, TILE, W), F32),
            pltpu.VMEM((2, W, TILE), F32),
            dma((5,)), dma((STAGES + 1, MODES)), dma((STAGES + 1, MODES)), dma((2, MODES)),
            dma((6,)), dma((6,)), dma((8,)), dma((4,)), dma((10,)), dma((10,)), dma((8,)), dma((4,)),
        ],
        compiler_params=pltpu.CompilerParams(collective_id=0, has_side_effects=True, vmem_limit_bytes=62 * 1024 * 1024),
        name="ptycho",
    )(row_offset, col_offset, live, object_field, probe, intensity, jnp.asarray(tables()), jnp.asarray(column_order()))
    return (object_grad, probe_grad)


def solution(mesh):
    in_specs = (
        P(None, "row", "col"),
        P(),
        P(("row", "col"), None, None),
        P(("row", "col")),
        P(("row", "col")),
        P(("row", "col")),
    )
    out_specs = (P(None, "row", "col"), P())
    return jax.shard_map(shards, mesh=mesh, in_specs=in_specs, out_specs=out_specs, check_vma=False)
```

```python
import functools
import jax
import jax.numpy as jnp
import numpy as np
from jax import lax
from jax.experimental import pallas as pl
from jax.experimental.pallas import tpu as pltpu
from jax.sharding import PartitionSpec as P

BF = jnp.bfloat16
F32 = jnp.float32
W, MODES, TILE, EXT, HALF = 256, 8, 512, 768, 128


def split_np(m):
    hi = m.astype(np.float32).astype(jnp.bfloat16)
    lo = (m - hi.astype(np.float64)).astype(np.float32).astype(jnp.bfloat16)
    return hi, lo


def tables():
    n = np.arange(HALF)
    out = []
    for odd in (0, 1):
        k = 2 * np.arange(HALF) + odd
        phase = 2.0 * np.pi * ((k[:, None] * n[None, :]) % W) / W
        c, s = np.cos(phase) / 16.0, np.sin(phase) / 16.0
        m = np.block([[c, s], [-s, c]])
        for t in (m, m.T):
            out.extend(split_np(t))
    return np.stack(out)


def column_order():
    q = np.zeros((W, W), np.float32)
    for j in range(HALF):
        q[2 * j, j] = 1.0
        q[2 * j + 1, HALF + j] = 1.0
    return np.stack([q, q.T]).astype(jnp.bfloat16)


def parts(x):
    hi = x.astype(BF)
    lo = (x - hi.astype(F32)).astype(BF)
    return hi, lo


def dot(a, b):
    return jnp.dot(a, b, preferred_element_type=F32)


def left(tab, i, data):
    hi, lo = parts(data)
    return dot(tab[i], hi) + dot(tab[i + 1], hi) + dot(tab[i], lo)


def right(data, tab, i):
    hi, lo = parts(data)
    return dot(hi, tab[i]) + dot(hi, tab[i + 1]) + dot(lo, tab[i])


ME, MET, MO, MOT = 0, 2, 4, 6


def transform(re, im, tab):
    even = jnp.concatenate([re[:HALF] + re[HALF:], im[:HALF] + im[HALF:]], 0)
    odd = jnp.concatenate([re[:HALF] - re[HALF:], im[:HALF] - im[HALF:]], 0)
    ye = left(tab, ME, even)
    yo = left(tab, MO, odd)
    a = jnp.concatenate([
        jnp.concatenate([y[:HALF, :HALF] + y[:HALF, HALF:], y[HALF:, :HALF] + y[HALF:, HALF:]], 1) for y in (ye, yo)], 0)
    b = jnp.concatenate([
        jnp.concatenate([y[:HALF, :HALF] - y[:HALF, HALF:], y[HALF:, :HALF] - y[HALF:, HALF:]], 1) for y in (ye, yo)], 0)
    return right(a, tab, MET), right(b, tab, MOT)


def inverse(fe, fo, tab):
    ge = right(fe, tab, ME)
    go = right(fo, tab, MO)
    p, q = ge + go, ge - go
    even = jnp.concatenate([
        jnp.concatenate([p[:HALF, :HALF], q[:HALF, :HALF]], 1),
        jnp.concatenate([p[:HALF, HALF:], q[:HALF, HALF:]], 1)], 0)
    odd = jnp.concatenate([
        jnp.concatenate([p[HALF:, :HALF], q[HALF:, :HALF]], 1),
        jnp.concatenate([p[HALF:, HALF:], q[HALF:, HALF:]], 1)], 0)
    a = left(tab, MET, even)
    b = left(tab, MOT, odd)
    s, d = a + b, a - b
    return jnp.concatenate([s[:HALF], d[:HALF]], 0), jnp.concatenate([s[HALF:], d[HALF:]], 0)


def picks(shape, axis, offset):
    a, b = lax.broadcasted_iota(jnp.int32, shape, axis), lax.broadcasted_iota(jnp.int32, shape, 1 - axis)
    return jnp.where(a - b == offset, 1.0, 0.0).astype(BF)


def select_left(sel, x):
    hi, lo = parts(x)
    return dot(sel, hi) + dot(sel, lo)


def select_right(x, sel):
    hi, lo = parts(x)
    return dot(hi, sel) + dot(lo, sel)


MESH = pl.DeviceIdType.MESH
N_ROW, N_COL = 8, 16
ROWS = 2 * W
STAGES = 13
OUT_STEPS = (0, -1)


def remote(src, dst, send, recv, to):
    return pltpu.make_async_remote_copy(src_ref=src, dst_ref=dst, send_sem=send, recv_sem=recv, device_id=to, device_id_type=MESH)


def count(flags):
    return sum(f.astype(jnp.int32) for f in flags)


def both(a, b):
    return jnp.logical_and(a, b)


def hypercube(row, col):
    z_hi, y = row // 4, row % 4
    z_lo, x, core = col // 8, col // 2 % 4, col % 2
    z = z_hi * 2 + z_lo

    def dev(x, y, z):
        return (z // 2 * 4 + y, z % 2 * 8 + x * 2 + core)

    def flip(p):
        return p + 1 - 2 * (p % 2)

    def gray(p):
        return (p + 1) // 2 % 2

    bits = [
        (gray(z),) + dev(x, y, flip(z)),
        (gray(x),) + dev(flip(x), y, z),
        (z // 2,) + dev(x, y, 3 - z),
        (x // 2,) + dev(3 - x, y, z),
    ]
    return bits, core, (row, col + 1 - 2 * core), y, dev(x, (y + 3) % 4, z), dev(x, (y + 1) % 4, z)


def relay_roles(row, col, source, step):
    core, z_lo, y = col % 2, col // 8, source % 4
    move = step[0] * (1 - core) + step[1] * core
    first = (source // 4 * 2 + 4 + move) % 4 // 2 * 4 + y
    second = (source // 4 * 2 + 5 + move) % 4 // 2 * 4 + y
    used = move != 0
    is_relay = jnp.logical_or(both(row == first, z_lo == 1), both(row == second, z_lo == 0))
    return both(used, row == source), both(used, row == 7 - source), both(used, is_relay), first * (1 - z_lo) + second * z_lo


def main_kernel(top_ref, col_ref, live_ref, obj, probe_hbm, int_hbm, tab_hbm, perm_hbm, own, total,
                ext, grad, mid, rows_of, cols_of, rows_to, cols_to, patch, spec, contrib, amp, probe, inten, tab, perm, pgm, first, data, later, gath, ring,
                hold_in, hold_out, add_c, add_r, add_l,
                lsem, asend, arecv, osem, isend, irecv, rsend, rrecv, hsend, hrecv, qsend, qrecv):
    row, col = lax.axis_index("row"), lax.axis_index("col")
    bits, core, twin, y, y_next, y_prev = hypercube(row, col)
    up, down, lft, rht = row > 0, row < N_ROW - 1, col > 0, col < N_COL - 1
    in_src, in_dst, in_relay, in_row = relay_roles(row, col, 4, (0, 1))
    out_src, out_dst, out_relay, out_row = relay_roles(row, col, 3, OUT_STEPS)
    swap = col + 8 - 16 * (col // 8)
    yes = row >= 0
    no_down, no_rht = jnp.logical_not(down), jnp.logical_not(rht)
    above, below = (lax.max(row - 1, 0), col), (lax.min(row + 1, N_ROW - 1), col)
    left, right = (row, lax.max(col - 1, 0)), (row, lax.min(col + 1, N_COL - 1))

    barrier = pltpu.get_barrier_semaphore()
    peers = [(up, above), (down, below), (lft, left), (rht, right), (yes, twin), (yes, y_next), (yes, y_prev)] + [(yes, b[1:]) for b in bits]
    peers += [(in_src, (in_row, swap)), (in_dst, (in_row, swap)), (in_relay, (4, swap)), (in_relay, (3, swap))]
    peers += [(out_src, (out_row, swap)), (out_dst, (out_row, swap)), (out_relay, (3, swap)), (out_relay, (4, swap))]
    for ok, dev in peers:
        @pl.when(ok)
        def _():
            pl.semaphore_signal(barrier, inc=1, device_id=dev, device_id_type=MESH)

    loads = [
        pltpu.make_async_copy(obj, ext.at[:, pl.ds(0, TILE), pl.ds(0, TILE)], lsem.at[0]),
        pltpu.make_async_copy(probe_hbm, probe, lsem.at[1]),
        pltpu.make_async_copy(tab_hbm, tab, lsem.at[2]),
        pltpu.make_async_copy(int_hbm, inten, lsem.at[3]),
        pltpu.make_async_copy(perm_hbm, perm, lsem.at[4]),
    ]
    pl.semaphore_wait(barrier, count([p[0] for p in peers]))

    pieces = [(c, j) for j in range(2) for c in range(2)]

    def cut(ref, i, start):
        c, j = pieces[i]
        return ref.at[c, pl.ds(start, W), pl.ds(j * W, W)]

    in_direct = [remote(cut(obj, i, 0), cut(ext, i, TILE), isend.at[i], irecv.at[i], above) for i in range(4)]
    in_hop = [remote(cut(obj, i, 0), cut(hold_in, i, 0), rsend.at[i], rrecv.at[i], (in_row, swap)) for i in range(4)]
    in_on = [remote(cut(hold_in, i, 0), cut(ext, i, TILE), rsend.at[4 + i], irecv.at[i], (3, swap)) for i in range(4)]
    side = remote(obj.at[:, :, pl.ds(0, W)], ext.at[:, pl.ds(0, TILE), pl.ds(TILE, W)], isend.at[4], irecv.at[4], left)
    corner = remote(ext.at[:, pl.ds(TILE, W), pl.ds(0, W)], ext.at[:, pl.ds(TILE, W), pl.ds(TILE, W)], isend.at[5], irecv.at[5], left)
    in_up = both(up, jnp.logical_not(in_src))

    @pl.when(in_src)
    def _():
        for c in in_hop:
            c.start()

    @pl.when(in_up)
    def _():
        for c in in_direct:
            c.start()

    @pl.when(lft)
    def _():
        side.start()

    for c in loads:
        c.start()

    @pl.when(no_down)
    def _():
        ext[:, pl.ds(TILE, W), :] = jnp.zeros((2, W, EXT), F32)

    @pl.when(no_rht)
    def _():
        ext[:, pl.ds(0, TILE), pl.ds(TILE, W)] = jnp.zeros((2, TILE, W), F32)
        ext[:, pl.ds(TILE, W), pl.ds(TILE, W)] = jnp.zeros((2, W, W), F32)

    for k in range(2):
        rows_of[pl.ds(k * W, W), :] = picks((W, EXT), 1, top_ref[k])
        cols_of[k] = picks((EXT, W), 0, col_ref[k])
        rows_to[:, pl.ds(k * W, W)] = picks((EXT, W), 0, top_ref[k])
        cols_to[k] = picks((W, EXT), 1, col_ref[k])
    contrib[...] = jnp.zeros_like(contrib)
    amp[...] = jnp.zeros_like(amp)
    for c in loads:
        c.wait()
    for k in range(2):
        hi, lo = parts(jnp.sqrt(inten[k]))
        hi, lo = dot(perm[1], hi).astype(BF), dot(perm[1], lo).astype(BF)
        inten[k] = dot(hi, perm[0]) + dot(lo, perm[0])

    def rows_own(j):
        for c in range(2):
            cols = pl.ds(j * W, W)
            mid[c, :, cols] = select_left(rows_of[:, :TILE], ext[c, pl.ds(0, TILE), cols])

    rows_own(0)
    rows_own(1)

    @pl.when(in_relay)
    def _():
        for i in range(4):
            in_hop[i].wait_recv()
            in_on[i].start()

    @pl.when(down)
    def _():
        in_direct[0].wait_recv()
        in_direct[1].wait_recv()

    @pl.when(both(down, lft))
    def _():
        corner.start()

    @pl.when(rht)
    def _():
        side.wait_recv()

    rows_own(2)

    @pl.when(down)
    def _():
        in_direct[2].wait_recv()
        in_direct[3].wait_recv()

    @pl.when(both(down, rht))
    def _():
        corner.wait_recv()

    for c in range(2):
        for j in range(3):
            cols = pl.ds(j * W, W)
            mid[c, :, cols] += select_left(rows_of[:, TILE:], ext[c, pl.ds(TILE, W), cols])
        for k in range(2):
            patch[k, c] = select_right(mid[c, pl.ds(k * W, W), :], cols_of[k])

    def forward(m, carry):
        pr, pi = probe[0, m], probe[1, m]
        for k in range(2):
            o_r, o_i = patch[k, 0], patch[k, 1]
            fe, fo = transform(pr * o_r - pi * o_i, pr * o_i + pi * o_r, tab)
            spec[k, m, 0] = fe
            spec[k, m, 1] = fo
            fe2, fo2 = fe * fe, fo * fo
            amp[k] += jnp.concatenate([fe2[:, :HALF] + fe2[:, HALF:], fo2[:, :HALF] + fo2[:, HALF:]], 1)
        return carry

    lax.fori_loop(0, MODES, forward, 0, unroll=2)
    for k in range(2):
        alive = live_ref[k].astype(F32)
        amp[k] = (1.0 - inten[k] / jnp.sqrt(amp[k] + 0.25)) * alive

    mine = pl.ds(pl.multiple_of(core * HALF, HALF), HALF)
    other = pl.ds(pl.multiple_of((1 - core) * HALF, HALF), HALF)

    def backward(m):
        pr, pi = probe[0, m], probe[1, m]
        gr = gi = None
        for k in range(2):
            o_r, o_i = patch[k, 0], patch[k, 1]
            f = amp[k]
            fe, fo = f[:, :HALF], f[:, HALF:]
            chi_r, chi_i = inverse(spec[k, m, 0] * jnp.concatenate([fe, fe], 1), spec[k, m, 1] * jnp.concatenate([fo, fo], 1), tab)
            contrib[k, 0] += pr * chi_r + pi * chi_i
            contrib[k, 1] += pr * chi_i - pi * chi_r
            qr = o_r * chi_r + o_i * chi_i
            qi = o_r * chi_i - o_i * chi_r
            gr = qr if gr is None else gr + qr
            gi = qi if gi is None else gi + qi
        pgm[m, pl.ds(0, W), :] = gr
        pgm[m, pl.ds(W, W), :] = gi

    def swap_copy(s):
        return remote(pgm.at[s, :, other], first.at[s], asend.at[0, s], arecv.at[0, s], twin)

    def halving_copy(i, s, off, to):
        n = ROWS >> (i + 1)
        return remote(data.at[s, pl.ds(pl.multiple_of(off, 8), n), :], later.at[s, pl.ds(ROWS - (ROWS >> i), n), :], asend.at[1 + i, s], arecv.at[1 + i, s], to)

    def merge(s):
        data[s] = pgm[s, :, mine] + first[s]

    def begin(s, bit):
        halving_copy(0, s, (1 - bit[0]) * W, bit[1:]).start()

    def tick(tau, turned):
        backward(tau)

        @pl.when(tau > 0)
        def _():
            swap_copy(tau - 1).wait()
            merge(tau - 1)
            begin(tau - 1, turned[3])

        swap_copy(tau).start()
        return turned[1:] + turned[:1]

    lax.fori_loop(0, MODES, tick, tuple(bits))

    def place(c):
        for k in range(2):
            mid[c, pl.ds(k * W, W), :] = select_right(contrib[k, c], cols_to[k])
        for j in range(3):
            cols = pl.ds(j * W, W)
            grad[c, :, cols] = select_left(rows_to[...], mid[c, :, cols])

    place(0)
    swap_copy(MODES - 1).wait()
    merge(MODES - 1)
    begin(MODES - 1, bits[(MODES - 1) % 4])
    offs = [[bits[s % 4][0] * W] for s in range(MODES)]
    flying = [halving_copy(0, s, (1 - bits[s % 4][0]) * W, bits[s % 4][1:]) for s in range(MODES)]

    def halve(i, streams=range(MODES)):
        for s in streams:
            n = ROWS >> i
            off = offs[s][-1]
            flying[s].wait()
            data[s, pl.ds(pl.multiple_of(off, 8), n), :] += later[s, pl.ds(ROWS - (ROWS >> (i - 1)), n), :]
            if i < 4:
                g, to = bits[(s + i) % 4][0], bits[(s + i) % 4][1:]
                flying[s] = halving_copy(i, s, off + (1 - g) * (n // 2), to)
                flying[s].start()
                offs[s].append(off + g * (n // 2))
            else:
                ring[3, s] = data[s, pl.ds(pl.multiple_of(off, 8), n), :]
                flying[s] = remote(ring.at[3, s], ring.at[0, s], asend.at[5, s], arecv.at[5, s], y_next)
                flying[s].start()

    halve(1, range(MODES - 1))
    place(1)

    h_corner = [remote(grad.at[c, pl.ds(TILE, W), pl.ds(TILE, W)], add_c.at[c], hsend.at[4 + c], hrecv.at[4 + c], right) for c in range(2)]
    h_side = [remote(grad.at[i // 2, pl.ds(i % 2 * W, W), pl.ds(TILE, W)], add_r.at[i // 2, pl.ds(i % 2 * W, W), :], hsend.at[6 + i], hrecv.at[6 + i], right) for i in range(4)]
    h_direct = [remote(cut(grad, i, TILE), cut(add_l, i, 0), hsend.at[i], hrecv.at[i], below) for i in range(4)]
    h_hop = [remote(cut(grad, i, TILE), cut(hold_out, i, 0), qsend.at[i], qrecv.at[i], (out_row, swap)) for i in range(4)]
    h_on = [remote(cut(hold_out, i, 0), cut(add_l, i, 0), qsend.at[4 + i], hrecv.at[i], (4, swap)) for i in range(4)]
    out_down = both(down, jnp.logical_not(out_src))

    def send_down(i):
        @pl.when(out_src)
        def _():
            h_hop[i].start()

        @pl.when(out_down)
        def _():
            h_direct[i].start()

    def send_side(*which):
        @pl.when(rht)
        def _():
            for i in which:
                h_side[i].start()

    def pass_on(*which):
        @pl.when(out_relay)
        def _():
            for i in which:
                h_hop[i].wait_recv()
                h_on[i].start()

    def turn_corner(c):
        @pl.when(both(down, lft))
        def _():
            h_corner[c].wait_recv()
            grad[c, pl.ds(TILE, W), pl.ds(0, W)] += add_c[c]

        send_down(c)

    def send_corner(c):
        @pl.when(both(down, rht))
        def _():
            h_corner[c].start()

    send_down(2)
    send_down(3)
    send_corner(0)


    def around(i):
        for s in range(MODES):
            flying[s].wait()
            flying[s] = remote(ring.at[i - 1, s], ring.at[i, s], asend.at[5 + i, s], arecv.at[5 + i, s], y_next)
            flying[s].start()

    def widen(i):
        n = ROWS >> (i + 1)
        for s in range(MODES):
            flying[s].wait()
            off = pl.multiple_of(offs[s][i], 8)
            if i == 3:
                gath[s, pl.ds(off, n), :] = ((ring[(3 - y) % 4, s] + ring[(4 - y) % 4, s]) + (ring[(5 - y) % 4, s] + ring[(6 - y) % 4, s]))
            here = gath.at[s, pl.ds(off, n), :]
            flying[s] = remote(here, here, asend.at[11 - i, s], arecv.at[11 - i, s], bits[(s + i) % 4][1:])
            flying[s].start()
            if i == 0:
                hand_over(s, 0)

    last = []

    def hand_over(s, second):
        c = 1 - bits[s % 4][0] if second else bits[s % 4][0]
        here, there = gath.at[s, pl.ds(pl.multiple_of(c * W, W), W), :], total.at[c, s, :, mine]
        pair = [remote(here, there, asend.at[12 + second, s], arecv.at[12 + second, s], twin), pltpu.make_async_copy(here, there, osem.at[second, s])]
        for d in pair:
            d.start()
        last.extend(pair)

    halve(1, [MODES - 1])
    halve(2)
    send_corner(1)
    halve(3)
    pass_on(2)
    halve(4)
    turn_corner(0)
    send_side(0)
    around(1)
    turn_corner(1)
    pass_on(3)
    send_side(1)
    around(2)
    send_side(2)
    pass_on(0)
    widen(3)
    pass_on(1)
    send_side(3)
    widen(2)
    widen(1)
    widen(0)
    for s in range(MODES):
        flying[s].wait()
        hand_over(s, 1)

    @pl.when(lft)
    def _():
        for i in range(4):
            h_side[i].wait_recv()
        grad[:, pl.ds(0, TILE), pl.ds(0, W)] += add_r[...]

    @pl.when(up)
    def _():
        for c in h_direct:
            c.wait_recv()
        grad[:, pl.ds(0, W), pl.ds(0, TILE)] += add_l[...]

    result = pltpu.make_async_copy(grad.at[:, pl.ds(0, TILE), pl.ds(0, TILE)], own, lsem.at[0])
    result.start()

    @pl.when(in_src)
    def _():
        for c in in_hop:
            c.wait_send()

    @pl.when(in_up)
    def _():
        for c in in_direct:
            c.wait_send()

    @pl.when(in_relay)
    def _():
        for c in in_on:
            c.wait_send()

    @pl.when(lft)
    def _():
        side.wait_send()

    @pl.when(both(down, lft))
    def _():
        corner.wait_send()

    @pl.when(both(down, rht))
    def _():
        for c in h_corner:
            c.wait_send()

    @pl.when(rht)
    def _():
        for c in h_side:
            c.wait_send()

    @pl.when(out_src)
    def _():
        for c in h_hop:
            c.wait_send()

    @pl.when(out_down)
    def _():
        for c in h_direct:
            c.wait_send()

    @pl.when(out_relay)
    def _():
        for c in h_on:
            c.wait_send()

    for c in last:
        c.wait()
    result.wait()


def shards(object_field, probe, intensity, row_offset, col_offset, live):
    smem = pl.BlockSpec(memory_space=pltpu.SMEM)
    hbm = pl.BlockSpec(memory_space=pl.ANY)
    dma = pltpu.SemaphoreType.DMA
    half = pltpu.VMEM((MODES, ROWS, HALF), F32)
    object_grad, probe_grad = pl.pallas_call(
        main_kernel,
        out_shape=(
            jax.ShapeDtypeStruct((2, TILE, TILE), F32),
            jax.ShapeDtypeStruct((2, MODES, W, W), F32),
        ),
        in_specs=[smem, smem, smem, hbm, hbm, hbm, hbm, hbm],
        out_specs=(hbm, hbm),
        scratch_shapes=[
            pltpu.VMEM((2, EXT, EXT), F32),
            pltpu.VMEM((2, EXT, EXT), F32),
            pltpu.VMEM((2, 2 * W, EXT), F32),
            pltpu.VMEM((2 * W, EXT), BF),
            pltpu.VMEM((2, EXT, W), BF),
            pltpu.VMEM((EXT, 2 * W), BF),
            pltpu.VMEM((2, W, EXT), BF),
            pltpu.VMEM((2, 2, W, W), F32),
            pltpu.VMEM((2, MODES, 2, W, W), F32),
            pltpu.VMEM((2, 2, W, W), F32),
            pltpu.VMEM((2, W, W), F32),
            pltpu.VMEM((2, MODES, W, W), F32),
            pltpu.VMEM((2, W, W), F32),
            pltpu.VMEM((8, W, W), BF),
            pltpu.VMEM((2, W, W), BF),
            pltpu.VMEM((MODES, ROWS, W), F32),
            half, half, half, half,
            pltpu.VMEM((4, MODES, ROWS // 16, HALF), F32),
            pltpu.VMEM((2, W, TILE), F32),
            pltpu.VMEM((2, W, TILE), F32),
            pltpu.VMEM((2, W, W), F32),
            pltpu.VMEM((2, TILE, W), F32),
            pltpu.VMEM((2, W, TILE), F32),
            dma((5,)), dma((STAGES + 1, MODES)), dma((STAGES + 1, MODES)), dma((2, MODES)),
            dma((6,)), dma((6,)), dma((8,)), dma((4,)), dma((10,)), dma((10,)), dma((8,)), dma((4,)),
        ],
        compiler_params=pltpu.CompilerParams(collective_id=0, has_side_effects=True, vmem_limit_bytes=62 * 1024 * 1024),
        name="ptycho",
    )(row_offset, col_offset, live, object_field, probe, intensity, jnp.asarray(tables()), jnp.asarray(column_order()))
    return (object_grad, probe_grad)


def solution(mesh):
    in_specs = (
        P(None, "row", "col"),
        P(),
        P(("row", "col"), None, None),
        P(("row", "col")),
        P(("row", "col")),
        P(("row", "col")),
    )
    out_specs = (P(None, "row", "col"), P())
    return jax.shard_map(shards, mesh=mesh, in_specs=in_specs, out_specs=out_specs, check_vma=False)
```
